32 devices in a mesh: grp: 2 (over x), col: 16 (over z, y, core).
Axes of the slice: x: 2, y: 2, z: 4, core: 2. Of those that a mesh axis runs over, the one named last changes fastest.
Arguments:
- mode_rows: float32 [16384, 256], P(('grp', 'col')), parts along dimension 0, may hold values from -8 to 8, as said below
- coeffs: bfloat16 [512, 256], P(('grp', 'col')), parts along dimension 0, may hold values from -18 to 18, as said below
- diffusivity: float32 [32, 64], P(('grp', 'col')), parts along dimension 0, may hold values from 0.02 to 0.24
- counts: int32 [32], P(('grp', 'col')), parts along dimension 0, may hold values from 32 to 64
- emis_idx: int32 [512], P('grp'), parts along dimension 0, may hold values from 0 to 15
- emis_table: float32 [16, 8], replicated, may hold values from 0.2 to 1.5
- reactants: int32 [12, 2], replicated, may hold values from 0 to 7
- stoich: int32 [12, 8], replicated, may hold values from -1 to 1
- rate_consts: float32 [12], replicated, may hold values from 0.02 to 0.2
- loss_rates: float32 [8], replicated, may hold values from 0.2 to 2
Outputs:
- modes_out: float32 [16384, 256], P(('grp', 'col')), parts along dimension 0
- coeffs_out: bfloat16 [512, 256], P(('grp', 'col')), parts along dimension 0
The draws below stay inside these ranges and needn't reach their ends.
There are 2 independent parts, one for each index of `grp`. The reference program is written for one: setup_inputs(seed, part) draws one part's arguments, and reference() takes and returns one part's arrays. A program takes and returns all parts, laid end to end along the dimension named above; an argument that names none is the same for every part. Nothing has to cross between parts.
Inputs may be any that keep to these rules, and one draw needn't show every extreme that they name: `mode_rows`: modes of order one. `coeffs`: coefficients of order one.
All inputs are finite; a program needn't handle non-finite values.
Results may differ from the reference program's by a relative error of at most 0.0014.
The reference program's roundings to bfloat16 on the way (of `mode_bf` and `tendency`) count: a program that leaves them out, or rounds other values in their place, can miss the bound.
Values may be sent and summed in bfloat16 or wider, within the bound.
No kernel may reach another device: no remote copies, remote signals or barrier semaphores. Data moves between devices by JAX's collectives and lax.ppermute only.
A program may use at most 64 MiB of HBM per device.

```python
import math
import jax
import jax.numpy as jnp
from jax import lax

S = 8
LEV = 64
R = 256
NREAC = 12
NEMIS = 16
NSUB = 2
COLUMNS = 16
ROWS = 8192
M = 256


def draw_mode_rows(key, part):
    noise_key, scale_key = jax.random.split(jax.random.fold_in(key, 11))
    row_rise = 0.5 + jnp.arange(ROWS, dtype=jnp.float32) / ROWS
    row_rough = jax.random.uniform(scale_key, (ROWS, 1), jnp.float32, 0.7, 1.3)
    base_draw = jnp.clip(jax.random.normal(noise_key, (ROWS, R), jnp.float32), -4.0, 4.0)
    return base_draw * row_rise[:, None] * row_rough


def draw_coeffs(key, part):
    noise_key, col_key, member_key = jax.random.split(jax.random.fold_in(key, 23), 3)
    col_scale = jnp.exp(jax.random.uniform(col_key, (R,), jnp.float32, jnp.log(0.3), jnp.log(3.0)))
    member_scale = jnp.exp(jax.random.uniform(member_key, (M,), jnp.float32, jnp.log(0.5), jnp.log(1.5)))
    base_draw = jnp.clip(jax.random.normal(noise_key, (M, R), jnp.float32), -4.0, 4.0)
    return (base_draw * col_scale[None, :] * member_scale[:, None]).astype(jnp.bfloat16)


def with_ends(array, key, least, high):
    dims = array.shape
    place = [jax.random.randint(jax.random.fold_in(key, axis), (), 0, dims[axis]) for axis in range(len(dims))]
    array = array.at[tuple(place)].set(least)
    longest = dims.index(max(dims))
    place[longest] = (place[longest] + 1) % dims[longest]
    return array.at[tuple(place)].set(high)


def block_levels(stream_key, extent, cuts, least, high):
    def one(dim, parts):
        draws = jax.random.uniform(jax.random.fold_in(jax.random.fold_in(stream_key, 6), dim), (parts,), jnp.float32, least / len(cuts), high / len(cuts))
        return jnp.repeat(jnp.exp(draws), extent[dim] // parts).reshape((-1,) + (1,) * (len(extent) - dim - 1))

    loudness = one(*cuts[0])
    for cut in cuts[1:]:
        loudness = loudness * one(*cut)
    return loudness


def setup_inputs(seed: int = 0, part: int = 0) -> dict:
    key_of = jax.random.split(jax.random.key(seed), 11)
    own_keys = jax.random.split(jax.random.fold_in(key_of[10], part), 11)
    mode_rows = draw_mode_rows(jax.random.fold_in(jax.random.fold_in(key_of[10], part), 71), part)
    coeffs = draw_coeffs(jax.random.fold_in(jax.random.fold_in(key_of[10], part), 71), part)
    diffusivity = jnp.clip(0.02 + 0.22 * jax.random.uniform(own_keys[2], (COLUMNS, LEV), jnp.float32) ** block_levels(own_keys[2], (COLUMNS, LEV), ((0, 16),), -0.2, 0.2), 0.02, 0.24)
    counts = with_ends(jax.random.randint(own_keys[3], (COLUMNS,), LEV // 2, LEV + 1), jax.random.fold_in(own_keys[3], 1), LEV // 2, LEV).astype(jnp.int32)
    emis_idx = with_ends(jax.random.randint(own_keys[4], (M,), 0, NEMIS), jax.random.fold_in(own_keys[4], 1), 0, NEMIS - 1).astype(jnp.int32)
    emis_table = jnp.clip(jax.random.uniform(key_of[5], (NEMIS, S), jnp.float32, 0.2, 1.5), 0.2, 1.5)
    reactants = with_ends(jax.random.randint(key_of[6], (NREAC, 2), 0, S), jax.random.fold_in(key_of[6], 1), 0, S - 1).astype(jnp.int32)
    stoich = with_ends(jax.random.randint(key_of[7], (NREAC, S), -1, 2), jax.random.fold_in(key_of[7], 1), -1, 1).astype(jnp.int32)
    rate_consts = jnp.clip(jnp.exp(jax.random.uniform(key_of[8], (NREAC,), jnp.float32, math.log(0.02), math.log(0.2))), 0.02, 0.2)
    loss_rates = jnp.clip(jnp.exp(jax.random.uniform(key_of[9], (S,), jnp.float32, math.log(0.2), math.log(2.0))), 0.2, 2.0)
    return dict(mode_rows=mode_rows, coeffs=coeffs, diffusivity=diffusivity, counts=counts, emis_idx=emis_idx, emis_table=emis_table, reactants=reactants, stoich=stoich, rate_consts=rate_consts, loss_rates=loss_rates)


TIME_STEP = 0.1
RATE_STEP = 0.3
RIDGE_SHARE = 0.05
PRECISE = lax.Precision.HIGHEST

def diffuse(mode_block, diffusivity, counts):
    ncols = counts.shape[0]
    rank = mode_block.shape[1]
    blocked = mode_block.reshape(ncols, S, LEV, rank)
    level_index = jnp.arange(LEV, dtype=jnp.int32)
    face_coef = jnp.where(level_index[None, :] + 1 < counts[:, None], diffusivity, jnp.zeros_like(diffusivity))
    upper_cells = jnp.concatenate([blocked[:, :, 1:], jnp.zeros_like(blocked[:, :, :1])], axis=2)
    face_flux = face_coef[:, None, :, None] * (upper_cells - blocked)
    lower_flux = jnp.concatenate([jnp.zeros_like(face_flux[:, :, :1]), face_flux[:, :, :-1]], axis=2)
    return (blocked + face_flux - lower_flux).reshape(mode_block.shape)

def reaction(field_block, reactants, stoich, rate_consts, loss_rates, emis_block, active, profile):
    first_amount = field_block[:, :, reactants[:, 0], :]
    second_amount = field_block[:, :, reactants[:, 1], :]
    reaction_speed = rate_consts[None, None, :, None] * first_amount * second_amount
    produced = jnp.einsum('rs,bcrl->bcsl', stoich.astype(jnp.float32), reaction_speed, precision=PRECISE)
    tendency_raw = produced - loss_rates[None, None, :, None] * field_block + emis_block[:, None, :, None] * profile[None, None, None, :]
    return tendency_raw * active[None, :, None, :]

def reference(mode_rows, coeffs, diffusivity, counts, emis_idx, emis_table, reactants, stoich, rate_consts, loss_rates):
    level_index = jnp.arange(LEV, dtype=jnp.int32)
    active = (level_index[None, :] < counts[:, None]).astype(jnp.float32)
    profile = jnp.exp(-4.0 * level_index.astype(jnp.float32) / LEV)
    member_emis = emis_table[emis_idx]
    ncols = counts.shape[0]
    rank_root = math.sqrt(R)
    inv_root = 1.0 / rank_root
    block_rows = math.gcd(M, 128)
    block_count = M // block_rows
    modes = mode_rows
    for substep in range(NSUB):
        diffused = diffuse(modes, diffusivity, counts)
        mode_bf = diffused.astype(jnp.bfloat16)

        def sweep_members(pulled, block_inputs):
            coef_block, emis_block = block_inputs
            field_block = lax.dot_general(coef_block.astype(jnp.float32), mode_bf.astype(jnp.float32), (((1,), (1,)), ((), ())), preferred_element_type=jnp.float32) * inv_root
            tendency = reaction(field_block.reshape(block_rows, ncols, S, LEV), reactants, stoich, rate_consts, loss_rates, emis_block, active, profile)
            tendency = tendency.reshape(block_rows, ROWS).astype(jnp.bfloat16)
            pulled = pulled + lax.dot_general(tendency.astype(jnp.float32), coef_block.astype(jnp.float32), (((0,), (0,)), ((), ())), preferred_element_type=jnp.float32)
            part_rate = jnp.dot(tendency.astype(jnp.float32), mode_bf.astype(jnp.float32), preferred_element_type=jnp.float32)
            return (pulled, part_rate)
        pulled, rate_blocks = lax.scan(sweep_members, jnp.zeros((ROWS, R), jnp.float32), (coeffs.reshape(block_count, block_rows, R), member_emis.reshape(block_count, block_rows, S)))
        coeff_rate = rate_blocks.reshape(M, R) * (rank_root / ROWS)
        coef_wide = coeffs.astype(jnp.float32)
        gram_matrix = jnp.dot(coef_wide.T, coef_wide, precision=PRECISE) + RIDGE_SHARE * M * jnp.eye(R, dtype=jnp.float32)
        proj_matrix = jnp.dot(mode_bf.astype(jnp.float32).T, pulled, precision=PRECISE) / ROWS
        remainder = pulled - jnp.dot(diffused, proj_matrix, precision=PRECISE)
        factor = jnp.linalg.cholesky(gram_matrix)
        solved = jax.scipy.linalg.cho_solve((factor, True), remainder.T).T
        modes = diffused + TIME_STEP * rank_root * solved
        coeffs = (coef_wide + RATE_STEP * coeff_rate).astype(jnp.bfloat16)
    return (modes, coeffs)
```

```python
import functools
import math

import jax
import jax.numpy as jnp
from jax import lax
from jax.experimental import pallas as pl
from jax.experimental.pallas import tpu as pltpu
from jax.sharding import PartitionSpec as P

S = 8
LEV = 64
R = 256
NREAC = 12
NEMIS = 16
NSUB = 2

TIME_STEP = 0.1
RATE_STEP = 0.3
RIDGE_SHARE = 0.05

F32 = jnp.float32
BF16 = jnp.bfloat16

NN = (((1,), (0,)), ((), ()))
NT = (((1,), (1,)), ((), ()))
TN = (((0,), (0,)), ((), ()))


def mm(a, b, dims=NN):
    return lax.dot_general(a, b, dims, preferred_element_type=F32)


def split(x):
    high = x.astype(BF16)
    return high, (x - high.astype(F32)).astype(BF16)


def mm3(a, b, dims=NN):
    return mm(a[0], b[0], dims) + (mm(a[0], b[1], dims) + mm(a[1], b[0], dims))


def diffuse_rows(modes, face_ref, counts_ref, columns):
    level = lax.broadcasted_iota(jnp.int32, (LEV, R), 0)
    faces = []
    for c in range(columns):
        face = jnp.broadcast_to(face_ref[:, c : c + 1], (LEV, R))
        faces += [jnp.where(level + 1 < counts_ref[c], face, 0.0)] * S
    face = jnp.concatenate(faces, axis=0)
    rows = modes.shape[0]
    flux = face * (pltpu.roll(modes, rows - 1, 0) - modes)
    return modes + flux - pltpu.roll(flux, 1, 0)


def react(
    diffused, coef_ref, emis_ref, counts_ref, pair_ref, stoich_ref, speed_ref, loss_ref,
    field_ref, tend_ref, rate_ref, columns,
):
    mode_bf = diffused.astype(BF16)
    members = coef_ref.shape[0]
    block = math.gcd(members, 256)
    step = 16
    steps = LEV // step
    for b in range(members // block):
        lanes = slice(b * block, (b + 1) * block)
        field_ref[...] = mm(mode_bf, coef_ref[lanes, :], NT) * (1.0 / math.sqrt(R))

        def part(i, _):
            c = i // steps
            low = (i - c * steps) * step
            base = c * (S * LEV) + low
            level = lax.broadcasted_iota(jnp.int32, (step, block), 0) + low
            profile = jnp.exp(level.astype(F32) * (-4.0 / LEV))
            live = level < counts_ref[c]

            def amount(s):
                return field_ref[pl.ds(pl.multiple_of(base + s * LEV, step), step), :]

            total = []
            for s in range(S):
                total.append(emis_ref[s : s + 1, lanes] * profile - loss_ref[s] * amount(s))
            for r in range(NREAC):
                speed = speed_ref[r] * amount(pair_ref[r, 0]) * amount(pair_ref[r, 1])
                for s in range(S):
                    total[s] = total[s] + stoich_ref[r, s].astype(F32) * speed
            for s in range(S):
                tend_ref[pl.ds(pl.multiple_of(base + s * LEV, step), step), lanes] = jnp.where(
                    live, total[s], 0.0
                ).astype(BF16)
            return 0

        lax.fori_loop(0, columns * steps, part, 0)
        rate_ref[lanes, :] = mm(tend_ref[:, lanes], mode_bf, TN)


def first_kernel(
    columns,
    counts_ref, pair_ref, stoich_ref, speed_ref, loss_ref, table_ref,
    modes_ref, face_ref, coef_ref, idx_ref,
    diff_ref, tend_ref, rate_ref, emis_ref,
    field_ref,
):
    index = idx_ref[...]
    for s in range(S):
        row = jnp.zeros(index.shape, F32)
        for k in range(NEMIS):
            row = jnp.where(index == k, table_ref[k, s], row)
        emis_ref[s : s + 1, :] = row
    diffused = diffuse_rows(modes_ref[...], face_ref, counts_ref, columns)
    diff_ref[...] = diffused
    react(
        diffused, coef_ref, emis_ref, counts_ref, pair_ref, stoich_ref, speed_ref, loss_ref,
        field_ref, tend_ref, rate_ref, columns,
    )


def advance(diffused, pull, solve_ref, rate):
    transfer = mm3(split(rate), split(solve_ref[...]), TN)
    moved = mm3(split(diffused), split(transfer))
    return diffused + (TIME_STEP * math.sqrt(R)) * (pull - moved)


def middle_kernel(
    columns, total_rows,
    counts_ref, pair_ref, stoich_ref, speed_ref, loss_ref,
    diff_in_ref, pull_ref, solve_ref, sum_ref, coef_ref, face_ref, emis_ref,
    diff_ref, tend_ref, rate_ref, coef_out_ref,
    field_ref,
):
    raw = sum_ref[...]
    coef_out_ref[...] = (
        coef_ref[...].astype(F32) + RATE_STEP * (raw * (math.sqrt(R) / total_rows))
    ).astype(BF16)
    modes = advance(diff_in_ref[...], pull_ref[...], solve_ref, raw * (1.0 / total_rows))
    diffused = diffuse_rows(modes, face_ref, counts_ref, columns)
    diff_ref[...] = diffused
    react(
        diffused, coef_out_ref, emis_ref, counts_ref, pair_ref, stoich_ref, speed_ref, loss_ref,
        field_ref, tend_ref, rate_ref, columns,
    )


def last_kernel(
    total_rows,
    place_ref,
    diff_in_ref, pull_ref, solve_ref, sum_ref, coef_ref,
    modes_ref, coef_out_ref,
):
    mine = coef_out_ref.shape[0]
    own = pl.ds(pl.multiple_of(place_ref[0] * mine, mine), mine)
    coef_out_ref[...] = (
        coef_ref[own, :].astype(F32)
        + RATE_STEP * (sum_ref[own, :] * (math.sqrt(R) / total_rows))
    ).astype(BF16)
    modes_ref[...] = advance(
        diff_in_ref[...], pull_ref[...], solve_ref, sum_ref[...] * (1.0 / total_rows)
    )


def solve_kernel(
    ridge, coef_ref, tend_ref, solve_ref, pull_ref, gram_high_ref, gram_low_ref, inv_ref
):
    coef = coef_ref[...]
    eye = (
        lax.broadcasted_iota(jnp.int32, (R, R), 0) == lax.broadcasted_iota(jnp.int32, (R, R), 1)
    ).astype(F32)
    gram = mm(coef, coef, TN) + ridge * eye
    top = jnp.max(jnp.sum(jnp.abs(gram), axis=0, keepdims=True))
    high, low = split(gram)
    gram_high_ref[...] = high
    gram_low_ref[...] = low
    scale = 2.0 / (top + ridge)
    inv_ref[...] = scale * eye
    gap = (top - ridge) / (top + ridge)

    def refine(gap):
        square = gap * gap
        factor = 2.0 / (2.0 - square)
        inv = inv_ref[...]
        halves = split(inv)
        rest = eye - mm3((gram_high_ref[...], gram_low_ref[...]), halves)
        inv_ref[...] = factor * (inv + mm3(halves, split(rest)))
        return square / (2.0 - square)

    lax.while_loop(lambda gap: gap > 1e-5, refine, gap)
    high, low = split(inv_ref[...])
    solve = mm(coef, high) + mm(coef, low)
    solve_ref[...] = solve
    high, low = split(solve)
    pull_ref[...] = mm(tend_ref[...], high) + mm(tend_ref[...], low)


VMEM_LIMIT = 48 * 1024 * 1024


def whole(n):
    return [pl.BlockSpec(memory_space=pltpu.VMEM)] * n


def scalars(n):
    return [pl.BlockSpec(memory_space=pltpu.SMEM)] * n


def call(kernel, n_scalar, outs, scratch, *args):
    return pl.pallas_call(
        kernel,
        in_specs=scalars(n_scalar) + whole(len(args) - n_scalar),
        out_specs=whole(len(outs)),
        out_shape=[jax.ShapeDtypeStruct(shape, dtype) for shape, dtype in outs],
        scratch_shapes=[pltpu.VMEM(shape, dtype) for shape, dtype in scratch],
        compiler_params=pltpu.CompilerParams(vmem_limit_bytes=VMEM_LIMIT),
    )(*args)


def sum_over(x, n):
    if n & (n - 1) or n < 2:
        return lax.psum(x, "col")

    def swap(value, mask):
        return lax.ppermute(value, "col", [(i, i ^ mask) for i in range(n)])

    half = x.shape[0] // 2
    side = lax.axis_index("col") & 1
    keep = lax.dynamic_slice_in_dim(x, side * half, half, 0)
    give = lax.dynamic_slice_in_dim(x, (1 - side) * half, half, 0)
    part = keep + swap(give, 1)
    mask = 2
    while mask < n:
        part = part + swap(part, mask if mask * 2 < n or mask < 8 else mask | (mask >> 1))
        mask *= 2
    other = swap(part, 1)
    return jnp.where(
        side == 0, jnp.concatenate([part, other], 0), jnp.concatenate([other, part], 0)
    )


def on_device(
    mode_rows,
    coeffs,
    diffusivity,
    counts,
    emis_idx,
    emis_table,
    reactants,
    stoich,
    rate_consts,
    loss_rates,
):
    n = lax.axis_size("col")
    rows = mode_rows.shape[0]
    total_rows = rows * n
    mine = coeffs.shape[0]
    members = mine * n
    columns = counts.shape[0]
    ridge = RIDGE_SHARE * members
    block = math.gcd(members, 256)
    place = lax.axis_index("col").astype(jnp.int32).reshape(1)
    face = diffusivity.T
    coef = lax.all_to_all(jnp.tile(coeffs, (n, 1)), "col", 0, 0, tiled=True)

    rows_f32 = ((rows, R), F32)
    tend_out = ((rows, members), BF16)
    rate_out = ((members, R), F32)
    field_tmp = ((rows, block), F32)
    chem = (counts, reactants, stoich, rate_consts, loss_rates)

    def solve(coef, tend):
        return call(
            functools.partial(solve_kernel, ridge), 0,
            [rate_out, rows_f32], [((R, R), BF16), ((R, R), BF16), ((R, R), F32)],
            coef, tend,
        )

    diff, tend, rate, emis = call(
        functools.partial(first_kernel, columns), 6,
        [rows_f32, tend_out, rate_out, ((S, members), F32)], [field_tmp],
        *chem, emis_table, mode_rows, face, coef, emis_idx.reshape(1, members),
    )
    for _ in range(NSUB - 1):
        total = sum_over(rate, n)
        solved, pull = solve(coef, tend)
        diff, tend, rate, coef = call(
            functools.partial(middle_kernel, columns, total_rows), 5,
            [rows_f32, tend_out, rate_out, ((members, R), BF16)], [field_tmp],
            *chem, diff, pull, solved, total, coef, face, emis,
        )
    total = sum_over(rate, n)
    solved, pull = solve(coef, tend)
    modes, coef_out = call(
        functools.partial(last_kernel, total_rows), 1,
        [rows_f32, ((mine, R), BF16)], [],
        place, diff, pull, solved, total, coef,
    )
    return (modes, coef_out)


def solution(mesh):
    placed = (
        P(("grp", "col"), None),
        P(("grp", "col"), None),
        P(("grp", "col"), None),
        P(("grp", "col")),
        P("grp"),
        P(),
        P(),
        P(),
        P(),
        P(),
    )
    return jax.shard_map(
        on_device,
        mesh=mesh,
        in_specs=placed,
        out_specs=(P(("grp", "col"), None), P(("grp", "col"), None)),
        check_vma=False,
    )
```

```python
import functools
import math

import jax
import jax.numpy as jnp
from jax import lax
from jax.experimental import pallas as pl
from jax.experimental.pallas import tpu as pltpu
from jax.sharding import PartitionSpec as P

S = 8
LEV = 64
R = 256
NREAC = 12
NEMIS = 16
NSUB = 2

TIME_STEP = 0.1
RATE_STEP = 0.3
RIDGE_SHARE = 0.05

F32 = jnp.float32
BF16 = jnp.bfloat16

NN = (((1,), (0,)), ((), ()))
NT = (((1,), (1,)), ((), ()))
TN = (((0,), (0,)), ((), ()))


def mm(a, b, dims=NN):
    return lax.dot_general(a, b, dims, preferred_element_type=F32)


def split(x):
    high = x.astype(BF16)
    return high, (x - high.astype(F32)).astype(BF16)


def mm3(a, b, dims=NN):
    return mm(a[0], b[0], dims) + (mm(a[0], b[1], dims) + mm(a[1], b[0], dims))


def diffuse_rows(modes, face_ref):
    faces = []
    for c in range(face_ref.shape[0] // LEV):
        faces += [face_ref[c * LEV : (c + 1) * LEV, :]] * S
    face = jnp.concatenate(faces, axis=0)
    rows = modes.shape[0]
    flux = face * (pltpu.roll(modes, rows - 1, 0) - modes)
    return modes + flux - pltpu.roll(flux, 1, 0)


def react(
    diffused, coef_ref, emis_ref, counts_ref, pair_ref, stoich_ref, speed_ref, loss_ref,
    field_ref, tend_ref, rate_ref, columns,
):
    mode_bf = diffused.astype(BF16)
    members = coef_ref.shape[0]
    block = math.gcd(members, 256)
    step = 16
    steps = LEV // step
    for b in range(members // block):
        lanes = slice(b * block, (b + 1) * block)
        field_ref[...] = mm(mode_bf, coef_ref[lanes, :], NT) * (1.0 / math.sqrt(R))

        def part(i, _):
            c = i // steps
            low = (i - c * steps) * step
            base = c * (S * LEV) + low
            level = lax.broadcasted_iota(jnp.int32, (step, block), 0) + low
            profile = jnp.exp(level.astype(F32) * (-4.0 / LEV))
            live = level < counts_ref[c]

            def amount(s):
                return field_ref[pl.ds(pl.multiple_of(base + s * LEV, step), step), :]

            total = []
            for s in range(S):
                total.append(emis_ref[s : s + 1, lanes] * profile - loss_ref[s] * amount(s))
            for r in range(NREAC):
                speed = speed_ref[r] * amount(pair_ref[0, r]) * amount(pair_ref[1, r])
                for s in range(S):
                    total[s] = total[s] + stoich_ref[s, r].astype(F32) * speed
            for s in range(S):
                tend_ref[pl.ds(pl.multiple_of(base + s * LEV, step), step), lanes] = jnp.where(
                    live, total[s], 0.0
                ).astype(BF16)
            return 0

        lax.fori_loop(0, columns * steps, part, 0)
        rate_ref[lanes, :] = mm(tend_ref[:, lanes], mode_bf, TN)


def setup_kernel(
    columns,
    counts_ref, table_ref,
    modes_ref, level_face_ref, idx_ref,
    diff_ref, emis_ref, face_ref,
):
    index = idx_ref[...]
    for s in range(S):
        row = jnp.zeros(index.shape, F32)
        for k in range(NEMIS):
            row = jnp.where(index == k, table_ref[s, k], row)
        emis_ref[s : s + 1, :] = row
    down = lax.broadcasted_iota(jnp.int32, (LEV, LEV), 0)
    across = lax.broadcasted_iota(jnp.int32, (LEV, LEV), 1)
    for c in range(columns):
        inner = (down == across) & (down + 1 < counts_ref[c])
        face = jnp.sum(jnp.where(inner, level_face_ref[c : c + 1, :], 0.0), axis=1, keepdims=True)
        face_ref[c * LEV : (c + 1) * LEV, :] = jnp.broadcast_to(face, (LEV, R))
    diff_ref[...] = diffuse_rows(modes_ref[...], face_ref)


def first_kernel(
    columns,
    counts_ref, pair_ref, stoich_ref, speed_ref, loss_ref,
    diff_ref, coef_ref, emis_ref,
    tend_ref, rate_ref,
    field_ref,
):
    react(
        diff_ref[...], coef_ref, emis_ref, counts_ref, pair_ref, stoich_ref, speed_ref, loss_ref,
        field_ref, tend_ref, rate_ref, columns,
    )


def advance(diffused, pull, solve_ref, rate):
    transfer = mm3(split(rate), split(solve_ref[...]), TN)
    moved = mm3(split(diffused), split(transfer))
    return diffused + (TIME_STEP * math.sqrt(R)) * (pull - moved)


def middle_kernel(
    columns, total_rows,
    counts_ref, pair_ref, stoich_ref, speed_ref, loss_ref,
    diff_in_ref, pull_ref, solve_ref, sum_ref, coef_ref, face_ref, emis_ref,
    diff_ref, tend_ref, rate_ref, coef_out_ref,
    field_ref,
):
    raw = sum_ref[...]
    coef_out_ref[...] = (
        coef_ref[...].astype(F32) + RATE_STEP * (raw * (math.sqrt(R) / total_rows))
    ).astype(BF16)
    modes = advance(diff_in_ref[...], pull_ref[...], solve_ref, raw * (1.0 / total_rows))
    diffused = diffuse_rows(modes, face_ref)
    diff_ref[...] = diffused
    react(
        diffused, coef_out_ref, emis_ref, counts_ref, pair_ref, stoich_ref, speed_ref, loss_ref,
        field_ref, tend_ref, rate_ref, columns,
    )


def last_kernel(
    total_rows,
    place_ref,
    diff_in_ref, pull_ref, solve_ref, sum_ref, coef_ref,
    modes_ref, coef_out_ref,
):
    mine = coef_out_ref.shape[0]
    own = pl.ds(pl.multiple_of(place_ref[0] * mine, mine), mine)
    coef_out_ref[...] = (
        coef_ref[own, :].astype(F32)
        + RATE_STEP * (sum_ref[own, :] * (math.sqrt(R) / total_rows))
    ).astype(BF16)
    modes_ref[...] = advance(
        diff_in_ref[...], pull_ref[...], solve_ref, sum_ref[...] * (1.0 / total_rows)
    )


def identity():
    return (
        lax.broadcasted_iota(jnp.int32, (R, R), 0) == lax.broadcasted_iota(jnp.int32, (R, R), 1)
    ).astype(F32)


def refine(eye, high_ref, low_ref, inv_ref, gap):
    square = gap * gap
    factor = 2.0 / (2.0 - square)
    inv = inv_ref[...]
    halves = split(inv)
    rest = eye - mm3((high_ref[...], low_ref[...]), halves)
    inv_ref[...] = factor * (inv + mm3(halves, split(rest)))
    return square / (2.0 - square)


def inverse_start(ridge, steps, coef_ref, high_ref, low_ref, inv_ref, gap_ref):
    coef = coef_ref[...]
    eye = identity()
    gram = mm(coef, coef, TN) + ridge * eye
    top = jnp.max(jnp.sum(jnp.abs(gram), axis=0, keepdims=True))
    high_ref[...], low_ref[...] = split(gram)
    inv_ref[...] = (2.0 / (top + ridge)) * eye
    gap = (top - ridge) / (top + ridge)
    gap_ref[0] = lax.fori_loop(
        0, steps, lambda i, gap: refine(eye, high_ref, low_ref, inv_ref, gap), gap
    )


def inverse_more(steps, gap_in_ref, high_ref, low_ref, inv_in_ref, inv_ref, gap_ref):
    eye = identity()
    inv_ref[...] = inv_in_ref[...]
    gap_ref[0] = lax.fori_loop(
        0, steps, lambda i, gap: refine(eye, high_ref, low_ref, inv_ref, gap), gap_in_ref[0]
    )


def inverse_end(
    gap_in_ref, high_ref, low_ref, inv_in_ref, coef_ref, tend_ref, solve_ref, pull_ref, inv_ref
):
    eye = identity()
    inv_ref[...] = inv_in_ref[...]
    lax.while_loop(
        lambda gap: gap > 1e-5,
        lambda gap: refine(eye, high_ref, low_ref, inv_ref, gap),
        gap_in_ref[0],
    )
    coef = coef_ref[...]
    high, low = split(inv_ref[...])
    solve = mm(coef, high) + mm(coef, low)
    solve_ref[...] = solve
    high, low = split(solve)
    pull_ref[...] = mm(tend_ref[...], high) + mm(tend_ref[...], low)


VMEM_LIMIT = 48 * 1024 * 1024


def whole(n):
    return [pl.BlockSpec(memory_space=pltpu.VMEM)] * n


def scalars(n):
    return [pl.BlockSpec(memory_space=pltpu.SMEM)] * n


SCALAR = "scalar"


def call(kernel, n_scalar, outs, scratch, *args):
    out_specs = []
    for out in outs:
        out_specs += scalars(1) if out is SCALAR else whole(1)
    return pl.pallas_call(
        kernel,
        in_specs=scalars(n_scalar) + whole(len(args) - n_scalar),
        out_specs=out_specs,
        out_shape=[
            jax.ShapeDtypeStruct(*(((1,), F32) if out is SCALAR else out)) for out in outs
        ],
        scratch_shapes=[pltpu.VMEM(shape, dtype) for shape, dtype in scratch],
        compiler_params=pltpu.CompilerParams(vmem_limit_bytes=VMEM_LIMIT),
    )(*args)


def sum_over(x, n, work):
    state = ()
    if n & (n - 1) or n < 4:
        for piece in work:
            state = piece(state)
        return lax.psum(x, "col"), state

    def swap(value, mask):
        return lax.ppermute(value, "col", [(i, i ^ mask) for i in range(n)])

    half = x.shape[0] // 2
    side = lax.axis_index("col") & 1
    keep = lax.dynamic_slice_in_dim(x, side * half, half, 0)
    give = lax.dynamic_slice_in_dim(x, (1 - side) * half, half, 0)
    part = keep + swap(give, 1)
    mask = 2
    work = list(work)
    while mask < n:
        last = mask * 2 >= n
        other = swap(part, mask if not last or mask < 8 else mask | (mask >> 1))
        while work:
            state = work.pop(0)(state, part)
            other, state = lax.optimization_barrier((other, state))
            if not last:
                break
        part = part + other
        mask *= 2
    other = swap(part, 1)
    total = jnp.where(
        side == 0, jnp.concatenate([part, other], 0), jnp.concatenate([other, part], 0)
    )
    return total, state


def on_device(
    mode_rows,
    coeffs,
    diffusivity,
    counts,
    emis_idx,
    emis_table,
    reactants,
    stoich,
    rate_consts,
    loss_rates,
):
    n = lax.axis_size("col")
    rows = mode_rows.shape[0]
    total_rows = rows * n
    mine = coeffs.shape[0]
    members = mine * n
    columns = counts.shape[0]
    ridge = RIDGE_SHARE * members
    block = math.gcd(members, 256)
    place = lax.axis_index("col").astype(jnp.int32).reshape(1)
    coef = lax.all_to_all(jnp.tile(coeffs, (n, 1)), "col", 0, 0, tiled=True)

    rows_f32 = ((rows, R), F32)
    tend_out = ((rows, members), BF16)
    rate_out = ((members, R), F32)
    field_tmp = ((rows, block), F32)
    square = ((R, R), F32)
    square_bf = ((R, R), BF16)
    chem = (counts, reactants.T, stoich.T, rate_consts, loss_rates)

    def summed(rate, coef, tend):
        def tied(part, *values):
            return lax.optimization_barrier((part, values))[1]

        def start(state, part):
            (first,) = tied(part, coef)
            return call(
                functools.partial(inverse_start, ridge, 3), 0,
                [square_bf, square_bf, square, SCALAR], [], first,
            )

        def more(state, part):
            high, low, inv, gap = tied(part, *state)
            inv, gap = call(
                functools.partial(inverse_more, 3), 1, [square, SCALAR], [], gap, high, low, inv
            )
            return high, low, inv, gap

        def end(state, part):
            high, low, inv, gap = tied(part, *state)
            return call(
                inverse_end, 1, [rate_out, rows_f32], [square], gap, high, low, inv, coef, tend
            )

        return sum_over(rate, n, (start, more, end))

    diff, emis, face = call(
        functools.partial(setup_kernel, columns), 2,
        [rows_f32, ((S, members), F32), ((columns * LEV, R), F32)], [],
        counts, emis_table.T, mode_rows, diffusivity, emis_idx.reshape(1, members),
    )
    tend, rate = call(
        functools.partial(first_kernel, columns), 5,
        [tend_out, rate_out], [field_tmp],
        *chem, diff, coef, emis,
    )
    for _ in range(NSUB - 1):
        total, (solved, pull) = summed(rate, coef, tend)
        diff, tend, rate, coef = call(
            functools.partial(middle_kernel, columns, total_rows), 5,
            [rows_f32, tend_out, rate_out, ((members, R), BF16)], [field_tmp],
            *chem, diff, pull, solved, total, coef, face, emis,
        )
    total, (solved, pull) = summed(rate, coef, tend)
    modes, coef_out = call(
        functools.partial(last_kernel, total_rows), 1,
        [rows_f32, ((mine, R), BF16)], [],
        place, diff, pull, solved, total, coef,
    )
    return (modes, coef_out)


def solution(mesh):
    placed = (
        P(("grp", "col"), None),
        P(("grp", "col"), None),
        P(("grp", "col"), None),
        P(("grp", "col")),
        P("grp"),
        P(),
        P(),
        P(),
        P(),
        P(),
    )
    return jax.shard_map(
        on_device,
        mesh=mesh,
        in_specs=placed,
        out_specs=(P(("grp", "col"), None), P(("grp", "col"), None)),
        check_vma=False,
    )
```

```python
import functools
import math

import jax
import jax.numpy as jnp
from jax import lax
from jax.experimental import pallas as pl
from jax.experimental.pallas import tpu as pltpu
from jax.sharding import PartitionSpec as P

S = 8
LEV = 64
R = 256
NREAC = 12
NEMIS = 16
NSUB = 2

TIME_STEP = 0.1
RATE_STEP = 0.3
RIDGE_SHARE = 0.05

F32 = jnp.float32
BF16 = jnp.bfloat16

NN = (((1,), (0,)), ((), ()))
NT = (((1,), (1,)), ((), ()))
TN = (((0,), (0,)), ((), ()))


def mm(a, b, dims=NN):
    return lax.dot_general(a, b, dims, preferred_element_type=F32)


def split(x):
    high = x.astype(BF16)
    return high, (x - high.astype(F32)).astype(BF16)


def mm3(a, b, dims=NN):
    return mm(a[0], b[0], dims) + (mm(a[0], b[1], dims) + mm(a[1], b[0], dims))


def diffuse_rows(modes, face_ref):
    faces = []
    for c in range(face_ref.shape[0] // LEV):
        faces += [face_ref[c * LEV : (c + 1) * LEV, :]] * S
    face = jnp.concatenate(faces, axis=0)
    rows = modes.shape[0]
    flux = face * (pltpu.roll(modes, rows - 1, 0) - modes)
    return modes + flux - pltpu.roll(flux, 1, 0)


def react(
    diffused, coef_ref, emis_ref, counts_ref, pair_ref, weight_ref,
    field_ref, tend_ref, rate_ref, top_ref, columns,
):
    mode_bf = diffused.astype(BF16)
    members = coef_ref.shape[0]
    block = math.gcd(members, 256)
    step = 16
    steps = LEV // step
    largest = jnp.full((1, R), 2.0**-120, F32)
    for b in range(members // block):
        lanes = slice(b * block, (b + 1) * block)
        field_ref[...] = mm(mode_bf, coef_ref[lanes, :], NT) * (1.0 / math.sqrt(R))

        def part(i, _):
            c = i // steps
            low = (i - c * steps) * step
            base = c * (S * LEV) + low
            level = lax.broadcasted_iota(jnp.int32, (step, block), 0) + low
            profile = jnp.exp(level.astype(F32) * (-4.0 / LEV))
            live = level < counts_ref[c]

            def amount(s):
                return field_ref[pl.ds(pl.multiple_of(base + s * LEV, step), step), :]

            total = []
            for s in range(S):
                total.append(emis_ref[s : s + 1, lanes] * profile - weight_ref[s, NREAC] * amount(s))
            for r in range(NREAC):
                speed = amount(pair_ref[0, r]) * amount(pair_ref[1, r])
                for s in range(S):
                    total[s] = total[s] + weight_ref[s, r] * speed
            for s in range(S):
                tend_ref[pl.ds(pl.multiple_of(base + s * LEV, step), step), lanes] = jnp.where(
                    live, total[s], 0.0
                ).astype(BF16)
            return 0

        lax.fori_loop(0, columns * steps, part, 0)
        rate = mm(tend_ref[:, lanes], mode_bf, TN)
        rate_ref[lanes, :] = rate
        largest = jnp.maximum(largest, jnp.max(jnp.abs(rate), axis=0, keepdims=True))
    power = jnp.maximum(jnp.floor(jnp.log(largest) * (1.0 / math.log(2.0))) + 2.0, -100.0)
    top_ref[...] = jnp.broadcast_to(power, top_ref.shape)


def setup_kernel(
    columns,
    counts_ref, table_ref,
    modes_ref, level_face_ref, idx_ref,
    diff_ref, emis_ref, face_ref,
):
    index = idx_ref[...]
    for s in range(S):
        row = jnp.zeros(index.shape, F32)
        for k in range(NEMIS):
            row = jnp.where(index == k, table_ref[s, k], row)
        emis_ref[s : s + 1, :] = row
    down = lax.broadcasted_iota(jnp.int32, (LEV, LEV), 0)
    across = lax.broadcasted_iota(jnp.int32, (LEV, LEV), 1)
    for c in range(columns):
        inner = (down == across) & (down + 1 < counts_ref[c])
        face = jnp.sum(jnp.where(inner, level_face_ref[c : c + 1, :], 0.0), axis=1, keepdims=True)
        face_ref[c * LEV : (c + 1) * LEV, :] = jnp.broadcast_to(face, (LEV, R))
    diff_ref[...] = diffuse_rows(modes_ref[...], face_ref)


def first_kernel(
    columns, plan,
    counts_ref, pair_ref, weight_ref,
    diff_ref, emis_ref, *refs,
):
    if plan:
        chip_ref, mine_ref, theirs_ref, tend_ref, rate_ref, top_ref, coef_ref, field_ref = refs
        rows = chip_ref.shape[0]
        place = lax.axis_index("col")
        chip, side = place // 2, place % 2
        for j, pair in enumerate(plan):
            for ref, mask in (
                (mine_ref, jnp.where(side == 0, pair[0], pair[1])),
                (theirs_ref, jnp.where(side == 0, pair[1], pair[0])),
            ):
                spot = pl.multiple_of((chip ^ mask) * rows, rows)
                coef_ref[pl.ds(spot, rows), :] = ref[j * rows : (j + 1) * rows, :]
        coef_ref[pl.ds(pl.multiple_of(chip * rows, rows), rows), :] = chip_ref[...]
    else:
        coef_ref, tend_ref, rate_ref, top_ref, field_ref = refs
    react(
        diff_ref[...], coef_ref, emis_ref, counts_ref, pair_ref, weight_ref,
        field_ref, tend_ref, rate_ref, top_ref, columns,
    )


def advance(diffused, pull, solve_ref, rate):
    transfer = mm3(split(rate), split(solve_ref[...]), TN)
    moved = mm3(split(diffused), split(transfer))
    return diffused + (TIME_STEP * math.sqrt(R)) * (pull - moved)


def middle_kernel(
    columns, total_rows,
    counts_ref, pair_ref, weight_ref,
    diff_in_ref, pull_ref, solve_ref, sum_ref, coef_ref, face_ref, emis_ref,
    diff_ref, tend_ref, rate_ref, top_ref, coef_out_ref,
    field_ref,
):
    raw = sum_ref[...]
    coef_out_ref[...] = (
        coef_ref[...].astype(F32) + RATE_STEP * (raw * (math.sqrt(R) / total_rows))
    ).astype(BF16)
    modes = advance(diff_in_ref[...], pull_ref[...], solve_ref, raw * (1.0 / total_rows))
    diffused = diffuse_rows(modes, face_ref)
    diff_ref[...] = diffused
    react(
        diffused, coef_out_ref, emis_ref, counts_ref, pair_ref, weight_ref,
        field_ref, tend_ref, rate_ref, top_ref, columns,
    )


def last_kernel(
    total_rows,
    diff_in_ref, pull_ref, solve_ref, sum_ref, coef_ref,
    modes_ref, coef_out_ref,
):
    mine = coef_out_ref.shape[0]
    own = pl.ds(pl.multiple_of(lax.axis_index("col") * mine, mine), mine)
    coef_out_ref[...] = (
        coef_ref[own, :].astype(F32)
        + RATE_STEP * (sum_ref[own, :] * (math.sqrt(R) / total_rows))
    ).astype(BF16)
    modes_ref[...] = advance(
        diff_in_ref[...], pull_ref[...], solve_ref, sum_ref[...] * (1.0 / total_rows)
    )


def identity():
    return (
        lax.broadcasted_iota(jnp.int32, (R, R), 0) == lax.broadcasted_iota(jnp.int32, (R, R), 1)
    ).astype(F32)


def refine(eye, high_ref, low_ref, inv_ref, gap):
    square = gap * gap
    factor = 2.0 / (2.0 - square)
    inv = inv_ref[...]
    halves = split(inv)
    rest = eye - mm3((high_ref[...], low_ref[...]), halves)
    inv_ref[...] = factor * (inv + mm3(halves, split(rest)))
    return square / (2.0 - square)


def inverse_start(ridge, steps, coef_ref, high_ref, low_ref, inv_ref, gap_ref):
    coef = coef_ref[...]
    eye = identity()
    gram = mm(coef, coef, TN) + ridge * eye
    top = jnp.max(jnp.sum(jnp.abs(gram), axis=0, keepdims=True))
    high_ref[...], low_ref[...] = split(gram)
    scale = 2.0 / (top + ridge)
    gap = (top - ridge) / (top + ridge)
    square = gap * gap
    factor = 2.0 / (2.0 - square)
    inv_ref[...] = (factor * scale) * (2.0 * eye - scale * gram)
    gap = lax.fori_loop(
        0, steps, lambda i, gap: refine(eye, high_ref, low_ref, inv_ref, gap),
        square / (2.0 - square),
    )
    gap_ref[...] = jnp.full(gap_ref.shape, gap, F32)


def inverse_end(
    gap_in_ref, high_ref, low_ref, inv_in_ref, coef_ref, tend_ref, solve_ref, pull_ref, inv_ref
):
    eye = identity()
    inv_ref[...] = inv_in_ref[...]
    lax.while_loop(
        lambda gap: gap > 1e-5,
        lambda gap: refine(eye, high_ref, low_ref, inv_ref, gap),
        jnp.max(gap_in_ref[...]),
    )
    coef = coef_ref[...]
    high, low = split(inv_ref[...])
    solve = mm(coef, high) + mm(coef, low)
    solve_ref[...] = solve
    high, low = split(solve)
    pull_ref[...] = mm(tend_ref[...], high) + mm(tend_ref[...], low)


VMEM_LIMIT = 48 * 1024 * 1024


def whole(n):
    return [pl.BlockSpec(memory_space=pltpu.VMEM)] * n


def scalars(n):
    return [pl.BlockSpec(memory_space=pltpu.SMEM)] * n


def call(kernel, n_scalar, outs, scratch, *args):
    return pl.pallas_call(
        kernel,
        in_specs=scalars(n_scalar) + whole(len(args) - n_scalar),
        out_specs=whole(len(outs)),
        out_shape=[jax.ShapeDtypeStruct(shape, dtype) for shape, dtype in outs],
        scratch_shapes=[pltpu.VMEM(shape, dtype) for shape, dtype in scratch],
        compiler_params=pltpu.CompilerParams(vmem_limit_bytes=VMEM_LIMIT),
    )(*args)


def tied(value, first):
    return lax.optimization_barrier((first, value))[1]


def swap(value, n, masks):
    return lax.ppermute(value, "col", [(i, i ^ masks[i % 2]) for i in range(n) if masks[i % 2]])


EXTRA = 8
LIFT = 15.0


def encode(part, power):
    scaled = (part * jnp.exp2(LIFT - power)).astype(jnp.float16)
    powers = jnp.broadcast_to(power, (EXTRA, R)).astype(jnp.float16)
    return lax.optimization_barrier(jnp.concatenate([scaled, powers], 0))


def decode(message):
    rows = message.shape[0] - EXTRA
    power = message[rows : rows + 1].astype(F32)
    return message[:rows].astype(F32) * jnp.exp2(power - LIFT), power


def sum_over(x, top, n, work):
    state = ()
    work = list(work)
    if n & (n - 1) or n < 4:
        while work:
            state = work.pop(0)(state, x)
        return lax.psum(x, "col"), state
    half = x.shape[0] // 2
    side = lax.axis_index("col") & 1
    keep = lax.dynamic_slice_in_dim(x, side * half, half, 0)
    give = lax.dynamic_slice_in_dim(x, (1 - side) * half, half, 0)
    got = swap(jnp.concatenate([give, top], 0), n, (1, 1))
    part = keep + got[:half]
    power = jnp.maximum(top[:1], got[half : half + 1]) + 1.0
    mask = 2
    while mask < n:
        masks = [mask, mask * 2, mask * 3] if mask * 2 < n else [mask]
        message = encode(part, power)
        others = [swap(message, n, (m, m)) for m in masks]
        mask *= 4 if len(masks) == 3 else 2
        while work:
            state = work.pop(0)(state, message)
            others, state = lax.optimization_barrier((others, state))
            if mask < n:
                break
        part, power = decode(message)
        for other in others:
            more, high = decode(other)
            part = part + more
            power = jnp.maximum(power, high)
        power = power + float(len(masks))
    other = swap(part, n, (1, 1))
    total = jnp.where(
        side == 0, jnp.concatenate([part, other], 0), jnp.concatenate([other, part], 0)
    )
    return total, state


def on_device(
    mode_rows,
    coeffs,
    diffusivity,
    counts,
    emis_idx,
    emis_table,
    reactants,
    stoich,
    rate_consts,
    loss_rates,
):
    n = lax.axis_size("col")
    rows = mode_rows.shape[0]
    total_rows = rows * n
    mine = coeffs.shape[0]
    members = mine * n
    columns = counts.shape[0]
    ridge = RIDGE_SHARE * members
    block = math.gcd(members, 256)
    rows_f32 = ((rows, R), F32)
    tend_out = ((rows, members), BF16)
    rate_out = ((members, R), F32)
    top_out = ((EXTRA, R), F32)
    coef_out = ((members, R), BF16)
    field_tmp = ((rows, block), F32)
    square = ((R, R), F32)
    square_bf = ((R, R), BF16)
    weights = stoich.astype(F32).T * rate_consts[None, :]
    chem = (counts, reactants.T, jnp.concatenate([weights, loss_rates[:, None]], 1))

    def setup(modes):
        return call(
            functools.partial(setup_kernel, columns), 2,
            [rows_f32, ((S, members), F32), ((columns * LEV, R), F32)], [],
            counts, emis_table.T, modes, diffusivity, emis_idx.reshape(1, members),
        )

    if n == 16:
        plan = ((1, 4), (2, 5), (3, 6), (0, 7))
        other = swap(coeffs, n, (1, 1))
        side = lax.axis_index("col") & 1
        chip = jnp.where(
            side == 0, jnp.concatenate([coeffs, other], 0), jnp.concatenate([other, coeffs], 0)
        )
        fetched = [swap(chip, n, (2 * a, 2 * b)) for a, b in plan]
        diff, emis, face = setup(tied(mode_rows, chip))
        fetched, diff = lax.optimization_barrier((fetched, diff))
        mine_rows = jnp.concatenate(fetched, 0)
        gathered = (chip, mine_rows, swap(mine_rows, n, (1, 1)))
        tend, rate, top, coef = call(
            functools.partial(first_kernel, columns, plan), 3,
            [tend_out, rate_out, top_out, coef_out], [field_tmp],
            *chem, diff, emis, *gathered,
        )
    else:
        coef = lax.all_to_all(jnp.tile(coeffs, (n, 1)), "col", 0, 0, tiled=True)
        diff, emis, face = setup(mode_rows)
        tend, rate, top = call(
            functools.partial(first_kernel, columns, ()), 3,
            [tend_out, rate_out, top_out], [field_tmp],
            *chem, diff, emis, coef,
        )

    def summed(rate, top, coef, tend):
        def start(state, ready):
            return call(
                functools.partial(inverse_start, ridge, 3), 0,
                [square_bf, square_bf, square, top_out], [], tied(coef, ready),
            )

        def end(state, ready):
            high, low, inv, gap = tied(state, ready)
            return call(
                inverse_end, 0, [rate_out, rows_f32], [square], gap, high, low, inv, coef, tend
            )

        return sum_over(rate, top, n, (start, end))

    for _ in range(NSUB - 1):
        total, (solved, pull) = summed(rate, top, coef, tend)
        diff, tend, rate, top, coef = call(
            functools.partial(middle_kernel, columns, total_rows), 3,
            [rows_f32, tend_out, rate_out, top_out, coef_out], [field_tmp],
            *chem, diff, pull, solved, total, coef, face, emis,
        )
    total, (solved, pull) = summed(rate, top, coef, tend)
    return tuple(
        call(
            functools.partial(last_kernel, total_rows), 0,
            [rows_f32, ((mine, R), BF16)], [],
            diff, pull, solved, total, coef,
        )
    )


def solution(mesh):
    placed = (
        P(("grp", "col"), None),
        P(("grp", "col"), None),
        P(("grp", "col"), None),
        P(("grp", "col")),
        P("grp"),
        P(),
        P(),
        P(),
        P(),
        P(),
    )
    return jax.shard_map(
        on_device,
        mesh=mesh,
        in_specs=placed,
        out_specs=(P(("grp", "col"), None), P(("grp", "col"), None)),
        check_vma=False,
    )
```

```python
import functools
import math

import jax
import jax.numpy as jnp
from jax import lax
from jax.experimental import pallas as pl
from jax.experimental.pallas import tpu as pltpu
from jax.sharding import PartitionSpec as P

S = 8
LEV = 64
R = 256
NREAC = 12
NEMIS = 16
NSUB = 2

TIME_STEP = 0.1
RATE_STEP = 0.3
RIDGE_SHARE = 0.05

F32 = jnp.float32
BF16 = jnp.bfloat16

NN = (((1,), (0,)), ((), ()))
NT = (((1,), (1,)), ((), ()))
TN = (((0,), (0,)), ((), ()))


def mm(a, b, dims=NN):
    return lax.dot_general(a, b, dims, preferred_element_type=F32)


def split(x):
    high = x.astype(BF16)
    return high, (x - high.astype(F32)).astype(BF16)


def mm3(a, b, dims=NN):
    return mm(a[0], b[0], dims) + (mm(a[0], b[1], dims) + mm(a[1], b[0], dims))


def diffuse_rows(modes, face_ref):
    faces = []
    for c in range(face_ref.shape[0] // LEV):
        faces += [face_ref[c * LEV : (c + 1) * LEV, :]] * S
    face = jnp.concatenate(faces, axis=0)
    rows = modes.shape[0]
    flux = face * (pltpu.roll(modes, rows - 1, 0) - modes)
    return modes + flux - pltpu.roll(flux, 1, 0)


def fetch(sources, targets, sems):
    copies = [
        pltpu.make_async_copy(source, target, sems.at[i])
        for i, (source, target) in enumerate(zip(sources, targets, strict=True))
    ]
    for copy in copies:
        copy.start()

    def wait():
        for copy in copies:
            copy.wait()

    return wait


def react(
    diffused, coef_ref, emis_ref, ready, counts_ref, pair_ref, stoich_ref, speed_ref, loss_ref,
    field_ref, tend_ref, rate_ref, top_ref, columns,
):
    mode_bf = diffused.astype(BF16)
    members = coef_ref.shape[0]
    block = math.gcd(members, 256)
    step = 16
    steps = LEV // step
    largest = jnp.full((1, R), 2.0**-120, F32)
    for b in range(members // block):
        lanes = slice(b * block, (b + 1) * block)
        field_ref[...] = mm(mode_bf, coef_ref[lanes, :], NT) * (1.0 / math.sqrt(R))
        if b == 0:
            ready()

        def part(i, _):
            c = i // steps
            low = (i - c * steps) * step
            base = c * (S * LEV) + low
            level = lax.broadcasted_iota(jnp.int32, (step, block), 0) + low
            profile = jnp.exp(level.astype(F32) * (-4.0 / LEV))
            live = level < counts_ref[c]

            def amount(s):
                return field_ref[pl.ds(pl.multiple_of(base + s * LEV, step), step), :]

            total = []
            for s in range(S):
                total.append(emis_ref[s : s + 1, lanes] * profile - loss_ref[s] * amount(s))
            for r in range(NREAC):
                speed = speed_ref[r] * amount(pair_ref[0, r]) * amount(pair_ref[1, r])
                for s in range(S):
                    total[s] = total[s] + stoich_ref[s, r].astype(F32) * speed
            for s in range(S):
                tend_ref[pl.ds(pl.multiple_of(base + s * LEV, step), step), lanes] = jnp.where(
                    live, total[s], 0.0
                ).astype(BF16)
            return 0

        lax.fori_loop(0, columns * steps, part, 0)
        rate = mm(tend_ref[:, lanes], mode_bf, TN)
        rate_ref[lanes, :] = rate
        largest = jnp.maximum(largest, jnp.max(jnp.abs(rate), axis=0, keepdims=True))
    power = jnp.maximum(jnp.floor(jnp.log(largest) * (1.0 / math.log(2.0))) + 2.0, -100.0)
    top_ref[...] = jnp.broadcast_to(power, top_ref.shape)


def stage_kernel(
    columns,
    counts_ref, table_hbm, level_face_hbm, idx_hbm, modes_hbm,
    modes_ref, emis_ref, face_ref,
    table_ref, level_face_ref, idx_ref, sems,
):
    modes_copy = pltpu.make_async_copy(modes_hbm, modes_ref, sems.at[3])
    modes_copy.start()
    fetch(
        (table_hbm, level_face_hbm, idx_hbm),
        (table_ref, level_face_ref, idx_ref),
        sems,
    )()
    index = idx_ref[...]
    for s in range(S):
        row = jnp.zeros(index.shape, F32)
        for k in range(NEMIS):
            row = jnp.where(index == k, table_ref[s, k], row)
        emis_ref[s : s + 1, :] = row
    down = lax.broadcasted_iota(jnp.int32, (LEV, LEV), 0)
    across = lax.broadcasted_iota(jnp.int32, (LEV, LEV), 1)
    for c in range(columns):
        inner = (down == across) & (down + 1 < counts_ref[c])
        face = jnp.sum(jnp.where(inner, level_face_ref[c : c + 1, :], 0.0), axis=1, keepdims=True)
        face_ref[c * LEV : (c + 1) * LEV, :] = jnp.broadcast_to(face, (LEV, R))
    modes_copy.wait()


def diffuse_kernel(modes_ref, face_ref, diff_ref):
    diff_ref[...] = diffuse_rows(modes_ref[...], face_ref)


def first_kernel(
    columns, plan,
    counts_ref, *allrefs,
):
    chem_hbm, chem, sems = allrefs[:4], allrefs[-5:-1], allrefs[-1]
    diff_ref, emis_ref, *refs, field_ref = allrefs[4:-5]
    ready = fetch(chem_hbm, chem, sems)
    if plan:
        chip_ref, mine_ref, theirs_ref, tend_ref, rate_ref, top_ref, coef_ref = refs
        rows = chip_ref.shape[0]
        place = lax.axis_index("col")
        chip, side = place // 2, place % 2
        for j, pair in enumerate(plan):
            for ref, mask in (
                (mine_ref, jnp.where(side == 0, pair[0], pair[1])),
                (theirs_ref, jnp.where(side == 0, pair[1], pair[0])),
            ):
                spot = pl.multiple_of((chip ^ mask) * rows, rows)
                coef_ref[pl.ds(spot, rows), :] = ref[j * rows : (j + 1) * rows, :]
        coef_ref[pl.ds(pl.multiple_of(chip * rows, rows), rows), :] = chip_ref[...]
    else:
        coef_ref, tend_ref, rate_ref, top_ref = refs
    react(
        diff_ref[...], coef_ref, emis_ref, ready, counts_ref, *chem,
        field_ref, tend_ref, rate_ref, top_ref, columns,
    )


def transfer_of(solve_ref, rate):
    return split(mm3(split(rate), split(solve_ref[...]), TN))


def advance(diffused, pull, transfer):
    moved = mm3(split(diffused), transfer)
    return diffused + (TIME_STEP * math.sqrt(R)) * (pull - moved)


def middle_kernel(
    columns, total_rows,
    counts_ref, pair_hbm, stoich_hbm, speed_hbm, loss_hbm,
    diff_in_ref, pull_ref, solve_ref, sum_ref, coef_ref, face_ref, emis_ref,
    diff_ref, tend_ref, rate_ref, top_ref, coef_out_ref,
    field_ref, *chem_sems,
):
    *chem, sems = chem_sems
    ready = fetch((pair_hbm, stoich_hbm, speed_hbm, loss_hbm), chem, sems)
    raw = sum_ref[...]
    coef_out_ref[...] = (
        coef_ref[...].astype(F32) + RATE_STEP * (raw * (math.sqrt(R) / total_rows))
    ).astype(BF16)
    transfer = transfer_of(solve_ref, raw * (1.0 / total_rows))
    modes = advance(diff_in_ref[...], pull_ref[...], transfer)
    diffused = diffuse_rows(modes, face_ref)
    diff_ref[...] = diffused
    react(
        diffused, coef_out_ref, emis_ref, ready, counts_ref, *chem,
        field_ref, tend_ref, rate_ref, top_ref, columns,
    )


def last_kernel(
    total_rows,
    diff_in_ref, pull_ref, solve_ref, sum_ref, coef_ref,
    modes_hbm, coef_out_ref,
    modes_ref, sems,
):
    mine = coef_out_ref.shape[0]
    own = pl.ds(pl.multiple_of(lax.axis_index("col") * mine, mine), mine)
    coef_out_ref[...] = (
        coef_ref[own, :].astype(F32)
        + RATE_STEP * (sum_ref[own, :] * (math.sqrt(R) / total_rows))
    ).astype(BF16)
    transfer = transfer_of(solve_ref, sum_ref[...] * (1.0 / total_rows))
    parts = sems.shape[0]
    rows = modes_ref.shape[0] // parts
    copies = []
    for i in range(parts):
        block = slice(i * rows, (i + 1) * rows)
        modes_ref[block, :] = advance(diff_in_ref[block, :], pull_ref[block, :], transfer)
        copies.append(
            pltpu.make_async_copy(
                modes_ref.at[pl.ds(i * rows, rows), :],
                modes_hbm.at[pl.ds(i * rows, rows), :],
                sems.at[i],
            )
        )
        copies[-1].start()
    for copy in copies:
        copy.wait()


def identity():
    return (
        lax.broadcasted_iota(jnp.int32, (R, R), 0) == lax.broadcasted_iota(jnp.int32, (R, R), 1)
    ).astype(F32)


def refine(eye, high_ref, low_ref, inv_ref, gap):
    square = gap * gap
    factor = 2.0 / (2.0 - square)
    inv = inv_ref[...]
    halves = split(inv)
    rest = eye - mm3((high_ref[...], low_ref[...]), halves)
    inv_ref[...] = factor * (inv + mm3(halves, split(rest)))
    return square / (2.0 - square)


def inverse_start(ridge, steps, coef_ref, high_ref, low_ref, inv_ref, gap_ref):
    coef = coef_ref[...]
    eye = identity()
    gram = mm(coef, coef, TN) + ridge * eye
    top = jnp.max(jnp.sum(jnp.abs(gram), axis=0, keepdims=True))
    high_ref[...], low_ref[...] = split(gram)
    scale = 2.0 / (top + ridge)
    gap = (top - ridge) / (top + ridge)
    square = gap * gap
    factor = 2.0 / (2.0 - square)
    inv_ref[...] = (factor * scale) * (2.0 * eye - scale * gram)
    gap = lax.fori_loop(
        0, steps, lambda i, gap: refine(eye, high_ref, low_ref, inv_ref, gap),
        square / (2.0 - square),
    )
    gap_ref[...] = jnp.full(gap_ref.shape, gap, F32)


def inverse_end(
    gap_in_ref, high_ref, low_ref, inv_in_ref, coef_ref, tend_ref, solve_ref, pull_ref, inv_ref
):
    eye = identity()
    inv_ref[...] = inv_in_ref[...]
    lax.while_loop(
        lambda gap: gap > 1e-5,
        lambda gap: refine(eye, high_ref, low_ref, inv_ref, gap),
        jnp.max(gap_in_ref[...]),
    )
    coef = coef_ref[...]
    high, low = split(inv_ref[...])
    solve = mm(coef, high) + mm(coef, low)
    solve_ref[...] = solve
    high, low = split(solve)
    pull_ref[...] = mm(tend_ref[...], high) + mm(tend_ref[...], low)


VMEM_LIMIT = 48 * 1024 * 1024


def call(kernel, n_hbm, outs, scratch, *args, counts=None, hbm_outs=0):
    def spaces(n, left):
        return [pl.BlockSpec(memory_space=pltpu.HBM if i < left else pltpu.VMEM) for i in range(n)]

    in_specs = spaces(len(args), n_hbm)
    args = [
        pltpu.with_memory_space_constraint(arg, pltpu.HBM) if i < n_hbm else arg
        for i, arg in enumerate(args)
    ]
    if counts is not None:
        in_specs = [pl.BlockSpec(memory_space=pltpu.SMEM)] + in_specs
        args = [counts] + args
    return pl.pallas_call(
        kernel,
        in_specs=in_specs,
        out_specs=spaces(len(outs), hbm_outs),
        out_shape=[jax.ShapeDtypeStruct(shape, dtype) for shape, dtype in outs],
        scratch_shapes=scratch,
        compiler_params=pltpu.CompilerParams(vmem_limit_bytes=VMEM_LIMIT),
    )(*args)


def tied(value, first):
    return lax.optimization_barrier((first, value))[1]


def swap(value, n, masks):
    return lax.ppermute(value, "col", [(i, i ^ masks[i % 2]) for i in range(n) if masks[i % 2]])


EXTRA = 8
LIFT = 15.0


def encode(part, power):
    scaled = (part * jnp.exp2(LIFT - power)).astype(jnp.float16)
    powers = jnp.broadcast_to(power, (EXTRA, R)).astype(jnp.float16)
    return lax.optimization_barrier(jnp.concatenate([scaled, powers], 0))


def decode(message):
    rows = message.shape[0] - EXTRA
    power = message[rows : rows + 1].astype(F32)
    return message[:rows].astype(F32) * jnp.exp2(power - LIFT), power


def sum_over(x, top, n, work):
    state = ()
    work = list(work)
    if n & (n - 1) or n < 4:
        while work:
            state = work.pop(0)(state, x)
        return lax.psum(x, "col"), state
    half = x.shape[0] // 2
    side = lax.axis_index("col") & 1
    keep = lax.dynamic_slice_in_dim(x, side * half, half, 0)
    give = lax.dynamic_slice_in_dim(x, (1 - side) * half, half, 0)
    got = swap(jnp.concatenate([give, top], 0), n, (1, 1))
    part = keep + got[:half]
    power = jnp.maximum(top[:1], got[half : half + 1]) + 1.0
    mask = 2
    while mask < n:
        masks = [mask, mask * 2, mask * 3] if mask * 2 < n else [mask]
        message = encode(part, power)
        others = [swap(message, n, (m, m)) for m in masks]
        mask *= 4 if len(masks) == 3 else 2
        while work:
            state = work.pop(0)(state, message)
            others, state = lax.optimization_barrier((others, state))
            if mask < n:
                break
        part, power = decode(message)
        for other in others:
            more, high = decode(other)
            part = part + more
            power = jnp.maximum(power, high)
        power = power + float(len(masks))
    other = swap(part, n, (1, 1))
    total = jnp.where(
        side == 0, jnp.concatenate([part, other], 0), jnp.concatenate([other, part], 0)
    )
    return total, state


def on_device(
    mode_rows,
    coeffs,
    diffusivity,
    counts,
    emis_idx,
    emis_table,
    reactants,
    stoich,
    rate_consts,
    loss_rates,
):
    n = lax.axis_size("col")
    rows = mode_rows.shape[0]
    total_rows = rows * n
    mine = coeffs.shape[0]
    members = mine * n
    columns = counts.shape[0]
    ridge = RIDGE_SHARE * members
    block = math.gcd(members, 256)
    rows_f32 = ((rows, R), F32)
    tend_out = ((rows, members), BF16)
    rate_out = ((members, R), F32)
    top_out = ((EXTRA, R), F32)
    coef_out = ((members, R), BF16)
    chem = (reactants.T, stoich.T, rate_consts, loss_rates)
    react_tmp = [
        pltpu.VMEM((rows, block), F32),
        *(pltpu.SMEM(value.shape, value.dtype) for value in chem),
        pltpu.SemaphoreType.DMA((len(chem),)),
    ]
    square = ((R, R), F32)
    square_bf = ((R, R), BF16)

    def stage(counts):
        index = emis_idx.reshape(1, members)
        return call(
            functools.partial(stage_kernel, columns), 4,
            [rows_f32, ((S, members), F32), ((columns * LEV, R), F32)],
            [
                pltpu.SMEM((S, NEMIS), F32),
                pltpu.VMEM(diffusivity.shape, F32),
                pltpu.VMEM((1, members), jnp.int32),
                pltpu.SemaphoreType.DMA((4,)),
            ],
            emis_table.T, diffusivity, index, mode_rows, counts=counts,
        )

    def spread(modes, face):
        return call(diffuse_kernel, 0, [rows_f32], [], modes, face)[0]

    if n == 16:
        plan = ((1, 2), (4, 3), (5, 6), (0, 7))
        other = swap(coeffs, n, (1, 1))
        modes, emis, face = stage(counts)
        other, modes = lax.optimization_barrier((other, modes))
        side = lax.axis_index("col") & 1
        chip = jnp.where(
            side == 0, jnp.concatenate([coeffs, other], 0), jnp.concatenate([other, coeffs], 0)
        )
        mine_rows = jnp.concatenate([swap(chip, n, (2 * a, 2 * b)) for a, b in plan], 0)
        theirs = swap(mine_rows, n, (1, 1))
        diff = spread(tied(modes, mine_rows), face)
        theirs, diff = lax.optimization_barrier((theirs, diff))
        gathered = (chip, mine_rows, theirs)
        tend, rate, top, coef = call(
            functools.partial(first_kernel, columns, plan), 4,
            [tend_out, rate_out, top_out, coef_out], react_tmp,
            *chem, diff, emis, *gathered, counts=counts,
        )
    else:
        coef = lax.all_to_all(jnp.tile(coeffs, (n, 1)), "col", 0, 0, tiled=True)
        modes, emis, face = stage(counts)
        diff = spread(modes, face)
        tend, rate, top = call(
            functools.partial(first_kernel, columns, ()), 4,
            [tend_out, rate_out, top_out], react_tmp,
            *chem, diff, emis, coef, counts=counts,
        )

    def summed(rate, top, coef, tend):
        def start(state, ready):
            return call(
                functools.partial(inverse_start, ridge, 3), 0,
                [square_bf, square_bf, square, top_out], [], tied(coef, ready),
            )

        def end(state, ready):
            high, low, inv, gap = tied(state, ready)
            return call(
                inverse_end, 0, [rate_out, rows_f32], [pltpu.VMEM((R, R), F32)], gap, high, low, inv, coef, tend
            )

        return sum_over(rate, top, n, (start, end))

    for _ in range(NSUB - 1):
        total, (solved, pull) = summed(rate, top, coef, tend)
        diff, tend, rate, top, coef = call(
            functools.partial(middle_kernel, columns, total_rows), 4,
            [rows_f32, tend_out, rate_out, top_out, coef_out], react_tmp,
            *chem, diff, pull, solved, total, coef, face, emis, counts=counts,
        )
    total, (solved, pull) = summed(rate, top, coef, tend)
    return tuple(
        call(
            functools.partial(last_kernel, total_rows), 0,
            [rows_f32, ((mine, R), BF16)],
            [pltpu.VMEM((rows, R), F32), pltpu.SemaphoreType.DMA((4,))],
            diff, pull, solved, total, coef, hbm_outs=1,
        )
    )


def solution(mesh):
    placed = (
        P(("grp", "col"), None),
        P(("grp", "col"), None),
        P(("grp", "col"), None),
        P(("grp", "col")),
        P("grp"),
        P(),
        P(),
        P(),
        P(),
        P(),
    )
    return jax.shard_map(
        on_device,
        mesh=mesh,
        in_specs=placed,
        out_specs=(P(("grp", "col"), None), P(("grp", "col"), None)),
        check_vma=False,
    )
```

```python
import functools
import math

import jax
import jax.numpy as jnp
from jax import lax
from jax.experimental import pallas as pl
from jax.experimental.pallas import tpu as pltpu
from jax.sharding import PartitionSpec as P

S = 8
LEV = 64
R = 256
NREAC = 12
NEMIS = 16
NSUB = 2

TIME_STEP = 0.1
RATE_STEP = 0.3
RIDGE_SHARE = 0.05

F32 = jnp.float32
BF16 = jnp.bfloat16

NN = (((1,), (0,)), ((), ()))
NT = (((1,), (1,)), ((), ()))
TN = (((0,), (0,)), ((), ()))


def mm(a, b, dims=NN):
    return lax.dot_general(a, b, dims, preferred_element_type=F32)


def split(x):
    high = x.astype(BF16)
    return high, (x - high.astype(F32)).astype(BF16)


def mm3(a, b, dims=NN):
    return mm(a[0], b[0], dims) + (mm(a[0], b[1], dims) + mm(a[1], b[0], dims))


def diffuse_rows(modes, face_ref):
    faces = []
    for c in range(face_ref.shape[0] // LEV):
        faces += [face_ref[c * LEV : (c + 1) * LEV, :]] * S
    face = jnp.concatenate(faces, axis=0)
    rows = modes.shape[0]
    flux = face * (pltpu.roll(modes, rows - 1, 0) - modes)
    return modes + flux - pltpu.roll(flux, 1, 0)


def fetch(sources, targets, sems):
    copies = [
        pltpu.make_async_copy(source, target, sems.at[i])
        for i, (source, target) in enumerate(zip(sources, targets, strict=True))
    ]
    for copy in copies:
        copy.start()

    def wait():
        for copy in copies:
            copy.wait()

    return wait


def react(
    diffused, coef_ref, emis_ref, live_ref, ready, pair_ref, stoich_ref, speed_ref, loss_ref,
    field_ref, tend_ref, rate_ref, top_ref, columns,
):
    mode_bf = diffused.astype(BF16)
    members = coef_ref.shape[0]
    block = math.gcd(members, 256)
    step = 16
    steps = LEV // step
    largest = jnp.full((1, R), 2.0**-120, F32)
    for b in range(members // block):
        lanes = slice(b * block, (b + 1) * block)
        field_ref[...] = mm(mode_bf, coef_ref[lanes, :], NT) * (1.0 / math.sqrt(R))
        if b == 0:
            ready()

        def part(i, _):
            c = i // steps
            low = (i - c * steps) * step
            base = c * (S * LEV) + low
            level = lax.broadcasted_iota(jnp.int32, (step, block), 0) + low
            profile = jnp.exp(level.astype(F32) * (-4.0 / LEV))
            live = live_ref[pl.ds(pl.multiple_of(c * LEV + low, step), step), 0:block] > 0.5

            def amount(s):
                return field_ref[pl.ds(pl.multiple_of(base + s * LEV, step), step), :]

            total = []
            for s in range(S):
                total.append(emis_ref[s : s + 1, lanes] * profile - loss_ref[0, s] * amount(s))
            for r in range(NREAC):
                speed = speed_ref[0, r] * amount(pair_ref[0, r]) * amount(pair_ref[1, r])
                for s in range(S):
                    total[s] = total[s] + stoich_ref[s, r].astype(F32) * speed
            for s in range(S):
                tend_ref[pl.ds(pl.multiple_of(base + s * LEV, step), step), lanes] = jnp.where(
                    live, total[s], 0.0
                ).astype(BF16)
            return 0

        lax.fori_loop(0, columns * steps, part, 0)
        rate = mm(tend_ref[:, lanes], mode_bf, TN)
        rate_ref[lanes, :] = rate
        largest = jnp.maximum(largest, jnp.max(jnp.abs(rate), axis=0, keepdims=True))
    power = jnp.maximum(jnp.floor(jnp.log(largest) * (1.0 / math.log(2.0))) + 2.0, -100.0)
    top_ref[...] = jnp.broadcast_to(power, top_ref.shape)


def stage_kernel(
    columns,
    pair_hbm, stoich_hbm, speed_hbm, loss_hbm, table_hbm, level_face_hbm, idx_hbm, modes_hbm,
    counts_ref,
    pair_ref, stoich_ref, speed_ref, loss_ref, modes_ref, emis_ref, face_ref, live_ref,
    table_ref, level_face_ref, idx_ref, sems,
):
    later = fetch(
        (pair_hbm, stoich_hbm, speed_hbm, loss_hbm, modes_hbm),
        (pair_ref, stoich_ref, speed_ref, loss_ref, modes_ref),
        sems,
    )
    fetch(
        (table_hbm, level_face_hbm, idx_hbm), (table_ref, level_face_ref, idx_ref), sems.at[5:8]
    )()
    index = idx_ref[...]
    for s in range(S):
        row = jnp.zeros(index.shape, F32)
        for k in range(NEMIS):
            row = jnp.where(index == k, table_ref[s, k], row)
        emis_ref[s : s + 1, :] = row
    down = lax.broadcasted_iota(jnp.int32, (LEV, LEV), 0)
    across = lax.broadcasted_iota(jnp.int32, (LEV, LEV), 1)
    level = lax.broadcasted_iota(jnp.int32, (LEV, R), 0)
    for c in range(columns):
        part = slice(c * LEV, (c + 1) * LEV)
        count = counts_ref[:, c : c + 1]
        inner = (down == across) & (down + 1 < count)
        face = jnp.sum(jnp.where(inner, level_face_ref[c : c + 1, :], 0.0), axis=1, keepdims=True)
        face_ref[part, :] = jnp.broadcast_to(face, (LEV, R))
        live_ref[part, :] = jnp.where(level < count, 1.0, 0.0)
    later()


def diffuse_kernel(modes_ref, face_ref, diff_ref):
    diff_ref[...] = diffuse_rows(modes_ref[...], face_ref)


def first_kernel(
    columns, plan,
    *allrefs,
):
    chem_in, chem, sems = allrefs[:4], allrefs[-5:-1], allrefs[-1]
    diff_ref, emis_ref, live_ref, *refs, field_ref = allrefs[4:-5]
    ready = fetch(chem_in, chem, sems)
    if plan:
        chip_ref, mine_ref, theirs_ref, tend_ref, rate_ref, top_ref, coef_ref = refs
        rows = chip_ref.shape[0]
        place = lax.axis_index("col")
        chip, side = place // 2, place % 2
        for j, pair in enumerate(plan):
            for ref, mask in (
                (mine_ref, jnp.where(side == 0, pair[0], pair[1])),
                (theirs_ref, jnp.where(side == 0, pair[1], pair[0])),
            ):
                spot = pl.multiple_of((chip ^ mask) * rows, rows)
                coef_ref[pl.ds(spot, rows), :] = ref[j * rows : (j + 1) * rows, :]
        coef_ref[pl.ds(pl.multiple_of(chip * rows, rows), rows), :] = chip_ref[...]
    else:
        coef_ref, tend_ref, rate_ref, top_ref = refs
    react(
        diff_ref[...], coef_ref, emis_ref, live_ref, ready, *chem,
        field_ref, tend_ref, rate_ref, top_ref, columns,
    )


def transfer_of(solve_ref, rate):
    return split(mm3(split(rate), split(solve_ref[...]), TN))


def advance(diffused, pull, transfer):
    moved = mm3(split(diffused), transfer)
    return diffused + (TIME_STEP * math.sqrt(R)) * (pull - moved)


def middle_kernel(
    columns, total_rows,
    pair_in_ref, stoich_in_ref, speed_in_ref, loss_in_ref,
    diff_in_ref, pull_ref, solve_ref, sum_ref, coef_ref, face_ref, emis_ref, live_ref,
    diff_ref, tend_ref, rate_ref, top_ref, coef_out_ref,
    field_ref, *chem_sems,
):
    *chem, sems = chem_sems
    ready = fetch((pair_in_ref, stoich_in_ref, speed_in_ref, loss_in_ref), chem, sems)
    raw = sum_ref[...]
    coef_out_ref[...] = (
        coef_ref[...].astype(F32) + RATE_STEP * (raw * (math.sqrt(R) / total_rows))
    ).astype(BF16)
    transfer = transfer_of(solve_ref, raw * (1.0 / total_rows))
    modes = advance(diff_in_ref[...], pull_ref[...], transfer)
    diffused = diffuse_rows(modes, face_ref)
    diff_ref[...] = diffused
    react(
        diffused, coef_out_ref, emis_ref, live_ref, ready, *chem,
        field_ref, tend_ref, rate_ref, top_ref, columns,
    )


def last_kernel(
    total_rows,
    diff_in_ref, pull_ref, solve_ref, sum_ref, coef_ref,
    modes_ref, coef_out_ref,
):
    mine = coef_out_ref.shape[0]
    own = pl.ds(pl.multiple_of(lax.axis_index("col") * mine, mine), mine)
    coef_out_ref[...] = (
        coef_ref[own, :].astype(F32)
        + RATE_STEP * (sum_ref[own, :] * (math.sqrt(R) / total_rows))
    ).astype(BF16)
    transfer = transfer_of(solve_ref, sum_ref[...] * (1.0 / total_rows))
    modes_ref[...] = advance(diff_in_ref[...], pull_ref[...], transfer)


def identity():
    return (
        lax.broadcasted_iota(jnp.int32, (R, R), 0) == lax.broadcasted_iota(jnp.int32, (R, R), 1)
    ).astype(F32)


def refine(eye, high_ref, low_ref, inv_ref, gap):
    square = gap * gap
    factor = 2.0 / (2.0 - square)
    inv = inv_ref[...]
    halves = split(inv)
    rest = eye - mm3((high_ref[...], low_ref[...]), halves)
    inv_ref[...] = factor * (inv + mm3(halves, split(rest)))
    return square / (2.0 - square)


def inverse_start(ridge, steps, coef_ref, high_ref, low_ref, inv_ref, gap_ref):
    coef = coef_ref[...]
    eye = identity()
    gram = mm(coef, coef, TN) + ridge * eye
    top = jnp.max(jnp.sum(jnp.abs(gram), axis=0, keepdims=True))
    high_ref[...], low_ref[...] = split(gram)
    scale = 2.0 / (top + ridge)
    gap = (top - ridge) / (top + ridge)
    square = gap * gap
    factor = 2.0 / (2.0 - square)
    inv_ref[...] = (factor * scale) * (2.0 * eye - scale * gram)
    gap = lax.fori_loop(
        0, steps, lambda i, gap: refine(eye, high_ref, low_ref, inv_ref, gap),
        square / (2.0 - square),
    )
    gap_ref[...] = jnp.full(gap_ref.shape, gap, F32)


def inverse_end(
    gap_in_ref, high_ref, low_ref, inv_in_ref, coef_ref, tend_ref, solve_ref, pull_ref, inv_ref
):
    eye = identity()
    inv_ref[...] = inv_in_ref[...]
    lax.while_loop(
        lambda gap: gap > 1e-5,
        lambda gap: refine(eye, high_ref, low_ref, inv_ref, gap),
        jnp.max(gap_in_ref[...]),
    )
    coef = coef_ref[...]
    high, low = split(inv_ref[...])
    solve = mm(coef, high) + mm(coef, low)
    solve_ref[...] = solve
    high, low = split(solve)
    pull_ref[...] = mm(tend_ref[...], high) + mm(tend_ref[...], low)


VMEM_LIMIT = 48 * 1024 * 1024


def call(kernel, n_hbm, outs, scratch, *args):
    args = [
        pltpu.with_memory_space_constraint(arg, pltpu.HBM) if i < n_hbm else arg
        for i, arg in enumerate(args)
    ]
    return pl.pallas_call(
        kernel,
        in_specs=[
            pl.BlockSpec(memory_space=pltpu.HBM if i < n_hbm else pltpu.VMEM)
            for i in range(len(args))
        ],
        out_specs=[pl.BlockSpec(memory_space=pltpu.VMEM)] * len(outs),
        out_shape=[jax.ShapeDtypeStruct(shape, dtype) for shape, dtype in outs],
        scratch_shapes=scratch,
        compiler_params=pltpu.CompilerParams(vmem_limit_bytes=VMEM_LIMIT),
    )(*args)


def tied(value, first):
    return lax.optimization_barrier((first, value))[1]


def swap(value, n, masks):
    return lax.ppermute(value, "col", [(i, i ^ masks[i % 2]) for i in range(n) if masks[i % 2]])


EXTRA = 8
LIFT = 15.0


def encode(part, power):
    scaled = (part * jnp.exp2(LIFT - power)).astype(jnp.float16)
    powers = jnp.broadcast_to(power, (EXTRA, R)).astype(jnp.float16)
    return lax.optimization_barrier(jnp.concatenate([scaled, powers], 0))


def decode(message):
    rows = message.shape[0] - EXTRA
    power = message[rows : rows + 1].astype(F32)
    return message[:rows].astype(F32) * jnp.exp2(power - LIFT), power


def sum_over(x, top, n, work):
    state = ()
    work = list(work)
    if n & (n - 1) or n < 4:
        while work:
            state = work.pop(0)(state, x)
        return lax.psum(x, "col"), state
    half = x.shape[0] // 2
    side = lax.axis_index("col") & 1
    keep = lax.dynamic_slice_in_dim(x, side * half, half, 0)
    give = lax.dynamic_slice_in_dim(x, (1 - side) * half, half, 0)
    got = swap(jnp.concatenate([give, top], 0), n, (1, 1))
    part = keep + got[:half]
    power = jnp.maximum(top[:1], got[half : half + 1]) + 1.0
    mask = 2
    while mask < n:
        masks = [mask, mask * 2, mask * 3] if mask * 2 < n else [mask]
        message = encode(part, power)
        others = [swap(message, n, (m, m)) for m in masks]
        mask *= 4 if len(masks) == 3 else 2
        while work:
            state = work.pop(0)(state, message)
            others, state = lax.optimization_barrier((others, state))
            if mask < n:
                break
        part, power = decode(message)
        for other in others:
            more, high = decode(other)
            part = part + more
            power = jnp.maximum(power, high)
        power = power + float(len(masks))
    other = swap(part, n, (1, 1))
    total = jnp.where(
        side == 0, jnp.concatenate([part, other], 0), jnp.concatenate([other, part], 0)
    )
    return total, state


def on_device(
    mode_rows,
    coeffs,
    diffusivity,
    counts,
    emis_idx,
    emis_table,
    reactants,
    stoich,
    rate_consts,
    loss_rates,
):
    n = lax.axis_size("col")
    rows = mode_rows.shape[0]
    total_rows = rows * n
    mine = coeffs.shape[0]
    members = mine * n
    columns = counts.shape[0]
    ridge = RIDGE_SHARE * members
    block = math.gcd(members, 256)
    rows_f32 = ((rows, R), F32)
    tend_out = ((rows, members), BF16)
    rate_out = ((members, R), F32)
    top_out = ((EXTRA, R), F32)
    coef_out = ((members, R), BF16)
    tables = (reactants.T, stoich.T, rate_consts.reshape(1, NREAC), loss_rates.reshape(1, S))
    react_tmp = [
        pltpu.VMEM((rows, block), F32),
        *(pltpu.SMEM(value.shape, value.dtype) for value in tables),
        pltpu.SemaphoreType.DMA((len(tables),)),
    ]
    square = ((R, R), F32)
    square_bf = ((R, R), BF16)

    def stage(modes):
        by_level = ((columns * LEV, R), F32)
        index = emis_idx.reshape(1, members)
        *chem, modes, emis, face, live = call(
            functools.partial(stage_kernel, columns), 8,
            [(value.shape, value.dtype) for value in tables]
            + [rows_f32, ((S, members), F32), by_level, by_level],
            [
                pltpu.SMEM((S, NEMIS), F32),
                pltpu.VMEM(diffusivity.shape, F32),
                pltpu.VMEM((1, members), jnp.int32),
                pltpu.SemaphoreType.DMA((8,)),
            ],
            *tables, emis_table.T, diffusivity, index, modes, counts.reshape(1, columns),
        )
        return chem, modes, emis, face, live

    def spread(modes, face):
        return call(diffuse_kernel, 0, [rows_f32], [], modes, face)[0]

    if n == 16:
        plan = ((1, 2), (4, 3), (5, 6), (0, 7))
        other = swap(coeffs, n, (1, 1))
        side = lax.axis_index("col") & 1
        chip = jnp.where(
            side == 0, jnp.concatenate([coeffs, other], 0), jnp.concatenate([other, coeffs], 0)
        )
        fetched = [swap(chip, n, (2 * a, 2 * b)) for a, b in plan]
        chem, modes, emis, face, live = stage(tied(mode_rows, chip))
        fetched, modes = lax.optimization_barrier((fetched, modes))
        mine_rows = jnp.concatenate(fetched, 0)
        theirs = swap(mine_rows, n, (1, 1))
        diff = spread(tied(modes, mine_rows), face)
        theirs, diff = lax.optimization_barrier((theirs, diff))
        gathered = (chip, mine_rows, theirs)
        tend, rate, top, coef = call(
            functools.partial(first_kernel, columns, plan), 0,
            [tend_out, rate_out, top_out, coef_out], react_tmp,
            *chem, diff, emis, live, *gathered,
        )
    else:
        coef = lax.all_to_all(jnp.tile(coeffs, (n, 1)), "col", 0, 0, tiled=True)
        chem, modes, emis, face, live = stage(mode_rows)
        diff = spread(modes, face)
        tend, rate, top = call(
            functools.partial(first_kernel, columns, ()), 0,
            [tend_out, rate_out, top_out], react_tmp,
            *chem, diff, emis, live, coef,
        )

    def summed(rate, top, coef, tend):
        def start(state, ready):
            return call(
                functools.partial(inverse_start, ridge, 3), 0,
                [square_bf, square_bf, square, top_out], [], tied(coef, ready),
            )

        def end(state, ready):
            high, low, inv, gap = tied(state, ready)
            return call(
                inverse_end, 0, [rate_out, rows_f32], [pltpu.VMEM((R, R), F32)], gap, high, low, inv, coef, tend
            )

        return sum_over(rate, top, n, (start, end))

    for _ in range(NSUB - 1):
        total, (solved, pull) = summed(rate, top, coef, tend)
        diff, tend, rate, top, coef = call(
            functools.partial(middle_kernel, columns, total_rows), 0,
            [rows_f32, tend_out, rate_out, top_out, coef_out], react_tmp,
            *chem, diff, pull, solved, total, coef, face, emis, live,
        )
    total, (solved, pull) = summed(rate, top, coef, tend)
    return tuple(
        call(
            functools.partial(last_kernel, total_rows), 0,
            [rows_f32, ((mine, R), BF16)], [],
            diff, pull, solved, total, coef,
        )
    )


def solution(mesh):
    placed = (
        P(("grp", "col"), None),
        P(("grp", "col"), None),
        P(("grp", "col"), None),
        P(("grp", "col")),
        P("grp"),
        P(),
        P(),
        P(),
        P(),
        P(),
    )
    return jax.shard_map(
        on_device,
        mesh=mesh,
        in_specs=placed,
        out_specs=(P(("grp", "col"), None), P(("grp", "col"), None)),
        check_vma=False,
    )
```

```python
import functools
import math

import jax
import jax.numpy as jnp
from jax import lax
from jax.experimental import pallas as pl
from jax.experimental.pallas import tpu as pltpu
from jax.sharding import PartitionSpec as P

S = 8
LEV = 64
R = 256
NREAC = 12
NEMIS = 16
NSUB = 2

TIME_STEP = 0.1
RATE_STEP = 0.3
RIDGE_SHARE = 0.05

F32 = jnp.float32
BF16 = jnp.bfloat16

NN = (((1,), (0,)), ((), ()))
NT = (((1,), (1,)), ((), ()))
TN = (((0,), (0,)), ((), ()))


def mm(a, b, dims=NN):
    return lax.dot_general(a, b, dims, preferred_element_type=F32)


def split(x):
    high = x.astype(BF16)
    return high, (x - high.astype(F32)).astype(BF16)


def mm3(a, b, dims=NN):
    return mm(a[0], b[0], dims) + (mm(a[0], b[1], dims) + mm(a[1], b[0], dims))


def diffuse_rows(modes, face_ref):
    faces = []
    for c in range(face_ref.shape[0] // LEV):
        faces += [face_ref[c * LEV : (c + 1) * LEV, :]] * S
    face = jnp.concatenate(faces, axis=0)
    rows = modes.shape[0]
    flux = face * (pltpu.roll(modes, rows - 1, 0) - modes)
    return modes + flux - pltpu.roll(flux, 1, 0)


def fetch(sources, targets, sems):
    copies = [
        pltpu.make_async_copy(source, target, sems.at[i])
        for i, (source, target) in enumerate(zip(sources, targets, strict=True))
    ]
    for copy in copies:
        copy.start()

    def wait():
        for copy in copies:
            copy.wait()

    return wait


def react(
    diffused, base, coef_ref, emis_ref, live_ref, ready, pair_ref, stoich_ref, speed_ref, loss_ref,
    field_ref, tend_ref, rate_ref, top_ref,
):
    mode_bf = diffused.astype(BF16)
    members = tend_ref.shape[1]
    block = field_ref.shape[1]
    columns = diffused.shape[0] // (S * LEV)
    step = 16
    steps = LEV // step
    largest = jnp.full((1, R), 2.0**-120, F32)
    for b in range(members // block):
        lanes = slice(b * block, (b + 1) * block)
        spot = pl.ds(pl.multiple_of(base + b * block, block), block)
        field_ref[...] = mm(mode_bf, coef_ref[spot, :], NT) * (1.0 / math.sqrt(R))
        if b == 0:
            ready()

        def part(i, _):
            c = i // steps
            low = (i - c * steps) * step
            first = c * (S * LEV) + low
            level = lax.broadcasted_iota(jnp.int32, (step, block), 0) + low
            profile = jnp.exp(level.astype(F32) * (-4.0 / LEV))
            live = live_ref[pl.ds(pl.multiple_of(c * LEV + low, step), step), 0:block] > 0.5

            def amount(s):
                return field_ref[pl.ds(pl.multiple_of(first + s * LEV, step), step), :]

            total = []
            for s in range(S):
                total.append(emis_ref[s : s + 1, spot] * profile - loss_ref[0, s] * amount(s))
            for r in range(NREAC):
                speed = speed_ref[0, r] * amount(pair_ref[0, r]) * amount(pair_ref[1, r])
                for s in range(S):
                    total[s] = total[s] + stoich_ref[s, r].astype(F32) * speed
            for s in range(S):
                tend_ref[pl.ds(pl.multiple_of(first + s * LEV, step), step), lanes] = jnp.where(
                    live, total[s], 0.0
                ).astype(BF16)
            return 0

        lax.fori_loop(0, columns * steps, part, 0, unroll=members <= block)
        rate = mm(tend_ref[:, lanes], mode_bf, TN)
        rate_ref[lanes, :] = rate
        largest = jnp.maximum(largest, jnp.max(jnp.abs(rate), axis=0, keepdims=True))
    power = jnp.maximum(jnp.floor(jnp.log(largest) * (1.0 / math.log(2.0))) + 2.0, -100.0)
    top_ref[...] = jnp.broadcast_to(power, top_ref.shape)


def half_start(members, keep):
    side = lax.axis_index("col") & 1
    return (side if keep else 1 - side) * members


def stage_kernel(
    columns,
    pair_hbm, stoich_hbm, speed_hbm, loss_hbm, table_hbm, level_face_hbm, idx_hbm, modes_hbm,
    counts_ref,
    pair_ref, stoich_ref, speed_ref, loss_ref, modes_ref, emis_ref, face_ref, live_ref,
    table_ref, level_face_ref, idx_ref, sems,
):
    later = fetch(
        (pair_hbm, stoich_hbm, speed_hbm, loss_hbm, modes_hbm),
        (pair_ref, stoich_ref, speed_ref, loss_ref, modes_ref),
        sems,
    )
    fetch(
        (table_hbm, level_face_hbm, idx_hbm), (table_ref, level_face_ref, idx_ref), sems.at[5:8]
    )()
    index = idx_ref[...]
    for s in range(S):
        row = jnp.zeros(index.shape, F32)
        for k in range(NEMIS):
            row = jnp.where(index == k, table_ref[s, k], row)
        emis_ref[s : s + 1, :] = row
    down = lax.broadcasted_iota(jnp.int32, (LEV, LEV), 0)
    across = lax.broadcasted_iota(jnp.int32, (LEV, LEV), 1)
    level = lax.broadcasted_iota(jnp.int32, (LEV, R), 0)
    for c in range(columns):
        part = slice(c * LEV, (c + 1) * LEV)
        count = counts_ref[:, c : c + 1]
        inner = (down == across) & (down + 1 < count)
        face = jnp.sum(jnp.where(inner, level_face_ref[c : c + 1, :], 0.0), axis=1, keepdims=True)
        face_ref[part, :] = jnp.broadcast_to(face, (LEV, R))
        live_ref[part, :] = jnp.where(level < count, 1.0, 0.0)
    later()


def diffuse_kernel(modes_ref, face_ref, diff_ref):
    diff_ref[...] = diffuse_rows(modes_ref[...], face_ref)


def first_kernel(plan, *allrefs):
    chem_in, chem, sems = allrefs[:4], allrefs[-5:-1], allrefs[-1]
    diff_ref, emis_ref, live_ref, *refs, field_ref = allrefs[4:-5]
    ready = fetch(chem_in, chem, sems)
    if plan:
        chip_ref, mine_ref, theirs_ref, tend_ref, rate_ref, top_ref, coef_ref = refs
        rows = chip_ref.shape[0]
        place = lax.axis_index("col")
        chip, side = place // 2, place % 2
        for j, pair in enumerate(plan):
            for ref, mask in (
                (mine_ref, jnp.where(side == 0, pair[0], pair[1])),
                (theirs_ref, jnp.where(side == 0, pair[1], pair[0])),
            ):
                spot = pl.multiple_of((chip ^ mask) * rows, rows)
                coef_ref[pl.ds(spot, rows), :] = ref[j * rows : (j + 1) * rows, :]
        coef_ref[pl.ds(pl.multiple_of(chip * rows, rows), rows), :] = chip_ref[...]
    else:
        coef_ref, tend_ref, rate_ref, top_ref = refs
    react(
        diff_ref[...], half_start(tend_ref.shape[1], False), coef_ref, emis_ref, live_ref,
        ready, *chem, field_ref, tend_ref, rate_ref, top_ref,
    )


def second_kernel(
    pair_in_ref, stoich_in_ref, speed_in_ref, loss_in_ref,
    diff_ref, emis_ref, live_ref, coef_ref,
    tend_ref, rate_ref, top_ref,
    field_ref, *chem_sems,
):
    *chem, sems = chem_sems
    ready = fetch((pair_in_ref, stoich_in_ref, speed_in_ref, loss_in_ref), chem, sems)
    react(
        diff_ref[...], half_start(tend_ref.shape[1], True), coef_ref, emis_ref, live_ref,
        ready, *chem, field_ref, tend_ref, rate_ref, top_ref,
    )


STEP = TIME_STEP * math.sqrt(R)


def ready_kernel(
    diff_ref, pull_ref, solve_ref, base_ref, diff_high_ref, diff_low_ref, high_ref, low_ref
):
    diffused = diff_ref[...]
    base_ref[...] = diffused + STEP * pull_ref[...]
    diff_high_ref[...], diff_low_ref[...] = split(diffused)
    high_ref[...], low_ref[...] = split(solve_ref[...])


def advance(base_ref, diff_high_ref, diff_low_ref, high_ref, low_ref, rate):
    transfer = mm3(split(rate), (high_ref[...], low_ref[...]), TN)
    moved = mm3((diff_high_ref[...], diff_low_ref[...]), split(transfer))
    return base_ref[...] - STEP * moved


def middle_kernel(
    total_rows,
    pair_in_ref, stoich_in_ref, speed_in_ref, loss_in_ref,
    base_ref, diff_high_ref, diff_low_ref, high_ref, low_ref,
    sum_ref, coef_ref, face_ref, emis_ref, live_ref,
    diff_ref, tend_ref, rate_ref, top_ref, coef_out_ref,
    field_ref, *chem_sems,
):
    *chem, sems = chem_sems
    ready = fetch((pair_in_ref, stoich_in_ref, speed_in_ref, loss_in_ref), chem, sems)
    raw = sum_ref[...]
    coef_out_ref[...] = (
        coef_ref[...].astype(F32) + RATE_STEP * (raw * (math.sqrt(R) / total_rows))
    ).astype(BF16)
    modes = advance(
        base_ref, diff_high_ref, diff_low_ref, high_ref, low_ref, raw * (1.0 / total_rows)
    )
    diffused = diffuse_rows(modes, face_ref)
    diff_ref[...] = diffused
    react(
        diffused, half_start(tend_ref.shape[1], False), coef_out_ref, emis_ref, live_ref,
        ready, *chem, field_ref, tend_ref, rate_ref, top_ref,
    )


def last_kernel(
    total_rows,
    base_ref, diff_high_ref, diff_low_ref, high_ref, low_ref,
    sum_ref, coef_ref,
    modes_ref, coef_out_ref,
):
    mine = coef_out_ref.shape[0]
    own = pl.ds(pl.multiple_of(lax.axis_index("col") * mine, mine), mine)
    coef_out_ref[...] = (
        coef_ref[own, :].astype(F32)
        + RATE_STEP * (sum_ref[own, :] * (math.sqrt(R) / total_rows))
    ).astype(BF16)
    modes_ref[...] = advance(
        base_ref, diff_high_ref, diff_low_ref, high_ref, low_ref,
        sum_ref[...] * (1.0 / total_rows),
    )


def identity():
    return (
        lax.broadcasted_iota(jnp.int32, (R, R), 0) == lax.broadcasted_iota(jnp.int32, (R, R), 1)
    ).astype(F32)


def refine(eye, high_ref, low_ref, inv_ref, gap):
    square = gap * gap
    factor = 2.0 / (2.0 - square)
    inv = inv_ref[...]
    halves = split(inv)
    rest = eye - mm3((high_ref[...], low_ref[...]), halves)
    inv_ref[...] = factor * (inv + mm3(halves, split(rest)))
    return square / (2.0 - square)


def inverse_start(ridge, steps, coef_ref, high_ref, low_ref, inv_ref, gap_ref):
    coef = coef_ref[...]
    eye = identity()
    gram = mm(coef, coef, TN) + ridge * eye
    top = jnp.max(jnp.sum(jnp.abs(gram), axis=0, keepdims=True))
    high_ref[...], low_ref[...] = split(gram)
    scale = 2.0 / (top + ridge)
    gap = (top - ridge) / (top + ridge)
    square = gap * gap
    factor = 2.0 / (2.0 - square)
    inv_ref[...] = (factor * scale) * (2.0 * eye - scale * gram)
    gap = lax.fori_loop(
        0, steps, lambda i, gap: refine(eye, high_ref, low_ref, inv_ref, gap),
        square / (2.0 - square),
    )
    gap_ref[...] = jnp.full(gap_ref.shape, gap, F32)


def inverse_end(
    gap_in_ref, high_ref, low_ref, inv_in_ref, coef_ref, give_ref, keep_ref,
    solve_ref, pull_ref, inv_ref,
):
    eye = identity()
    inv_ref[...] = inv_in_ref[...]
    lax.while_loop(
        lambda gap: gap > 1e-5,
        lambda gap: refine(eye, high_ref, low_ref, inv_ref, gap),
        jnp.max(gap_in_ref[...]),
    )
    coef = coef_ref[...]
    high, low = split(inv_ref[...])
    solve = mm(coef, high) + mm(coef, low)
    solve_ref[...] = solve
    half = give_ref.shape[1]
    parts = []
    for ref, keep in ((give_ref, False), (keep_ref, True)):
        start = pl.multiple_of(half_start(half, keep), half)
        high, low = split(solve_ref[pl.ds(start, half), :])
        parts.append(mm(ref[...], high) + mm(ref[...], low))
    pull_ref[...] = parts[0] + parts[1]


VMEM_LIMIT = 48 * 1024 * 1024


def call(kernel, n_hbm, outs, scratch, *args):
    args = [
        pltpu.with_memory_space_constraint(arg, pltpu.HBM) if i < n_hbm else arg
        for i, arg in enumerate(args)
    ]
    return pl.pallas_call(
        kernel,
        in_specs=[
            pl.BlockSpec(memory_space=pltpu.HBM if i < n_hbm else pltpu.VMEM)
            for i in range(len(args))
        ],
        out_specs=[pl.BlockSpec(memory_space=pltpu.VMEM)] * len(outs),
        out_shape=[jax.ShapeDtypeStruct(shape, dtype) for shape, dtype in outs],
        scratch_shapes=scratch,
        compiler_params=pltpu.CompilerParams(vmem_limit_bytes=VMEM_LIMIT),
    )(*args)


def tied(value, first):
    return lax.optimization_barrier((first, value))[1]


def swap(value, n, masks):
    return lax.ppermute(value, "col", [(i, i ^ masks[i % 2]) for i in range(n) if masks[i % 2]])


EXTRA = 8
LIFT = 15.0


def encode(part, power):
    scaled = (part * jnp.exp2(LIFT - power)).astype(jnp.float16)
    powers = jnp.broadcast_to(power, (EXTRA, R)).astype(jnp.float16)
    return lax.optimization_barrier(jnp.concatenate([scaled, powers], 0))


def decode(message):
    rows = message.shape[0] - EXTRA
    power = message[rows : rows + 1].astype(F32)
    return message[:rows].astype(F32) * jnp.exp2(power - LIFT), power


def sum_over(give, top, keep_half, n, work, prepare):
    got = swap(jnp.concatenate([give, top], 0), n, (1, 1))
    keep, keep_top, state = keep_half()
    got, keep = lax.optimization_barrier((got, keep))
    half = give.shape[0]
    side = lax.axis_index("col") & 1
    part = keep + got[:half]
    power = jnp.maximum(keep_top[:1], got[half : half + 1]) + 1.0
    work = list(work)
    mask = 2
    while mask < n:
        masks = [mask, mask * 2, mask * 3] if mask * 2 < n else [mask]
        message = encode(part, power)
        others = [swap(message, n, (m, m)) for m in masks]
        mask *= 4 if len(masks) == 3 else 2
        while work:
            state = work.pop(0)(state, message)
            others, state = lax.optimization_barrier((others, state))
            if mask < n:
                break
        part, power = decode(message)
        for other in others:
            more, high = decode(other)
            part = part + more
            power = jnp.maximum(power, high)
        power = power + float(len(masks))
    other = swap(part, n, (1, 1))
    state = prepare(state, part)
    other, state = lax.optimization_barrier((other, state))
    total = jnp.where(
        side == 0, jnp.concatenate([part, other], 0), jnp.concatenate([other, part], 0)
    )
    return total, state


def on_device(
    mode_rows,
    coeffs,
    diffusivity,
    counts,
    emis_idx,
    emis_table,
    reactants,
    stoich,
    rate_consts,
    loss_rates,
):
    n = lax.axis_size("col")
    rows = mode_rows.shape[0]
    total_rows = rows * n
    mine = coeffs.shape[0]
    members = mine * n
    columns = counts.shape[0]
    ridge = RIDGE_SHARE * members
    half = members // 2
    block = math.gcd(half, 256)
    rows_f32 = ((rows, R), F32)
    rows_bf = ((rows, R), BF16)
    tend_out = ((rows, half), BF16)
    half_out = ((half, R), F32)
    rate_out = ((members, R), F32)
    top_out = ((EXTRA, R), F32)
    coef_out = ((members, R), BF16)
    tables = (reactants.T, stoich.T, rate_consts.reshape(1, NREAC), loss_rates.reshape(1, S))
    react_tmp = [
        pltpu.VMEM((rows, block), F32),
        *(pltpu.SMEM(value.shape, value.dtype) for value in tables),
        pltpu.SemaphoreType.DMA((len(tables),)),
    ]
    square = ((R, R), F32)
    square_bf = ((R, R), BF16)

    def stage(modes):
        by_level = ((columns * LEV, R), F32)
        index = emis_idx.reshape(1, members)
        *chem, modes, emis, face, live = call(
            functools.partial(stage_kernel, columns), 8,
            [(value.shape, value.dtype) for value in tables]
            + [rows_f32, ((S, members), F32), by_level, by_level],
            [
                pltpu.SMEM((S, NEMIS), F32),
                pltpu.VMEM(diffusivity.shape, F32),
                pltpu.VMEM((1, members), jnp.int32),
                pltpu.SemaphoreType.DMA((8,)),
            ],
            *tables, emis_table.T, diffusivity, index, modes, counts.reshape(1, columns),
        )
        return chem, modes, emis, face, live

    def spread(modes, face):
        return call(diffuse_kernel, 0, [rows_f32], [], modes, face)[0]

    if n == 16:
        plan = ((1, 2), (4, 3), (5, 6), (0, 7))
        other = swap(coeffs, n, (1, 1))
        side = lax.axis_index("col") & 1
        chip = jnp.where(
            side == 0, jnp.concatenate([coeffs, other], 0), jnp.concatenate([other, coeffs], 0)
        )
        fetched = [swap(chip, n, (2 * a, 2 * b)) for a, b in plan]
        chem, modes, emis, face, live = stage(tied(mode_rows, chip))
        fetched, modes = lax.optimization_barrier((fetched, modes))
        mine_rows = jnp.concatenate(fetched, 0)
        theirs = swap(mine_rows, n, (1, 1))
        diff = spread(tied(modes, mine_rows), face)
        theirs, diff = lax.optimization_barrier((theirs, diff))
        gathered = (chip, mine_rows, theirs)
        tend, rate, top, coef = call(
            functools.partial(first_kernel, plan), 0,
            [tend_out, half_out, top_out, coef_out], react_tmp,
            *chem, diff, emis, live, *gathered,
        )
    else:
        coef = lax.all_to_all(jnp.tile(coeffs, (n, 1)), "col", 0, 0, tiled=True)
        chem, modes, emis, face, live = stage(mode_rows)
        diff = spread(modes, face)
        tend, rate, top = call(
            functools.partial(first_kernel, ()), 0,
            [tend_out, half_out, top_out], react_tmp,
            *chem, diff, emis, live, coef,
        )

    def summed(rate, top, coef, tend, diff):
        def keep_half():
            tend_keep, keep, keep_top = call(
                second_kernel, 0, [tend_out, half_out, top_out], react_tmp,
                *chem, tied(diff, rate), emis, live, coef,
            )
            return keep, keep_top, tend_keep

        def start(tend_keep, ready):
            return tend_keep, call(
                functools.partial(inverse_start, ridge, 4), 0,
                [square_bf, square_bf, square, top_out], [], tied(coef, ready),
            )

        def end(state, ready):
            tend_keep, (high, low, inv, gap) = tied(state, ready)
            return call(
                inverse_end, 0, [rate_out, rows_f32], [pltpu.VMEM((R, R), F32)],
                gap, high, low, inv, coef, tend, tend_keep,
            )

        def prepare(state, ready):
            solved, pull = tied(state, ready)
            return call(
                ready_kernel, 0,
                [rows_f32, rows_bf, rows_bf, ((members, R), BF16), ((members, R), BF16)], [],
                diff, pull, solved,
            )

        return sum_over(rate, top, keep_half, n, (start, end), prepare)

    for _ in range(NSUB - 1):
        total, prepared = summed(rate, top, coef, tend, diff)
        diff, tend, rate, top, coef = call(
            functools.partial(middle_kernel, total_rows), 0,
            [rows_f32, tend_out, half_out, top_out, coef_out], react_tmp,
            *chem, *prepared, total, coef, face, emis, live,
        )
    total, prepared = summed(rate, top, coef, tend, diff)
    return tuple(
        call(
            functools.partial(last_kernel, total_rows), 0,
            [rows_f32, ((mine, R), BF16)], [],
            *prepared, total, coef,
        )
    )


def solution(mesh):
    placed = (
        P(("grp", "col"), None),
        P(("grp", "col"), None),
        P(("grp", "col"), None),
        P(("grp", "col")),
        P("grp"),
        P(),
        P(),
        P(),
        P(),
        P(),
    )
    return jax.shard_map(
        on_device,
        mesh=mesh,
        in_specs=placed,
        out_specs=(P(("grp", "col"), None), P(("grp", "col"), None)),
        check_vma=False,
    )
```

```python
import functools
import math

import jax
import jax.numpy as jnp
from jax import lax
from jax.experimental import pallas as pl
from jax.experimental.pallas import tpu as pltpu
from jax.sharding import PartitionSpec as P

S = 8
LEV = 64
R = 256
NREAC = 12
NEMIS = 16
NSUB = 2

TIME_STEP = 0.1
RATE_STEP = 0.3
RIDGE_SHARE = 0.05

F32 = jnp.float32
BF16 = jnp.bfloat16

NN = (((1,), (0,)), ((), ()))
NT = (((1,), (1,)), ((), ()))
TN = (((0,), (0,)), ((), ()))


def mm(a, b, dims=NN):
    return lax.dot_general(a, b, dims, preferred_element_type=F32)


def split(x):
    high = x.astype(BF16)
    return high, (x - high.astype(F32)).astype(BF16)


def mm3(a, b, dims=NN):
    return mm(a[0], b[0], dims) + (mm(a[0], b[1], dims) + mm(a[1], b[0], dims))


def diffuse_rows(modes, face_ref):
    faces = []
    for c in range(face_ref.shape[0] // LEV):
        faces += [face_ref[c * LEV : (c + 1) * LEV, :]] * S
    face = jnp.concatenate(faces, axis=0)
    rows = modes.shape[0]
    flux = face * (pltpu.roll(modes, rows - 1, 0) - modes)
    return modes + flux - pltpu.roll(flux, 1, 0)


def fetch(sources, targets, sems):
    copies = [
        pltpu.make_async_copy(source, target, sems.at[i])
        for i, (source, target) in enumerate(zip(sources, targets, strict=True))
    ]
    for copy in copies:
        copy.start()

    def wait():
        for copy in copies:
            copy.wait()

    return wait


def react(
    diffused, base, coef_base, coef_ref, emis_ref, live_ref, ready, pair_ref, stoich_ref, speed_ref, loss_ref,
    field_ref, tend_ref, rate_ref, top_ref,
):
    mode_bf = diffused.astype(BF16)
    members = tend_ref.shape[1]
    block = field_ref.shape[1]
    columns = diffused.shape[0] // (S * LEV)
    step = 16
    steps = LEV // step
    largest = jnp.full((1, R), 2.0**-120, F32)
    for b in range(members // block):
        lanes = slice(b * block, (b + 1) * block)
        spot = pl.ds(pl.multiple_of(base + b * block, block), block)
        member = pl.ds(pl.multiple_of(coef_base + b * block, block), block)
        field_ref[...] = mm(mode_bf, coef_ref[member, :], NT) * (1.0 / math.sqrt(R))
        if b == 0:
            ready()

        def part(i, _):
            c = i // steps
            low = (i - c * steps) * step
            first = c * (S * LEV) + low
            level = lax.broadcasted_iota(jnp.int32, (step, block), 0) + low
            profile = jnp.exp(level.astype(F32) * (-4.0 / LEV))
            live = live_ref[pl.ds(pl.multiple_of(c * LEV + low, step), step), 0:block] > 0.5

            def amount(s):
                return field_ref[pl.ds(pl.multiple_of(first + s * LEV, step), step), :]

            total = []
            for s in range(S):
                total.append(emis_ref[s : s + 1, spot] * profile - loss_ref[0, s] * amount(s))
            for r in range(NREAC):
                speed = speed_ref[0, r] * amount(pair_ref[0, r]) * amount(pair_ref[1, r])
                for s in range(S):
                    total[s] = total[s] + stoich_ref[s, r].astype(F32) * speed
            for s in range(S):
                tend_ref[pl.ds(pl.multiple_of(first + s * LEV, step), step), lanes] = jnp.where(
                    live, total[s], 0.0
                ).astype(BF16)
            return 0

        lax.fori_loop(0, columns * steps, part, 0, unroll=members <= block)
        rate = mm(tend_ref[:, lanes], mode_bf, TN)
        rate_ref[lanes, :] = rate
        largest = jnp.maximum(largest, jnp.max(jnp.abs(rate), axis=0, keepdims=True))
    power = jnp.maximum(jnp.floor(jnp.log(largest) * (1.0 / math.log(2.0))) + 2.0, -100.0)
    top_ref[...] = jnp.broadcast_to(power, top_ref.shape)


def half_start(members, keep):
    side = lax.axis_index("col") & 1
    return (side if keep else 1 - side) * members


def stage_kernel(
    columns,
    pair_hbm, stoich_hbm, speed_hbm, loss_hbm, table_hbm, level_face_hbm, idx_hbm, modes_hbm,
    counts_ref,
    pair_ref, stoich_ref, speed_ref, loss_ref, diff_ref, emis_ref, face_ref, live_ref,
    table_ref, level_face_ref, idx_ref, modes_ref, sems,
):
    later = fetch(
        (pair_hbm, stoich_hbm, speed_hbm, loss_hbm, modes_hbm),
        (pair_ref, stoich_ref, speed_ref, loss_ref, modes_ref),
        sems,
    )
    fetch(
        (table_hbm, level_face_hbm, idx_hbm), (table_ref, level_face_ref, idx_ref), sems.at[5:8]
    )()
    index = idx_ref[...]
    for s in range(S):
        row = jnp.zeros(index.shape, F32)
        for k in range(NEMIS):
            row = jnp.where(index == k, table_ref[s, k], row)
        emis_ref[s : s + 1, :] = row
    down = lax.broadcasted_iota(jnp.int32, (LEV, LEV), 0)
    across = lax.broadcasted_iota(jnp.int32, (LEV, LEV), 1)
    level = lax.broadcasted_iota(jnp.int32, (LEV, R), 0)
    for c in range(columns):
        part = slice(c * LEV, (c + 1) * LEV)
        count = counts_ref[:, c : c + 1]
        inner = (down == across) & (down + 1 < count)
        face = jnp.sum(jnp.where(inner, level_face_ref[c : c + 1, :], 0.0), axis=1, keepdims=True)
        face_ref[part, :] = jnp.broadcast_to(face, (LEV, R))
        live_ref[part, :] = jnp.where(level < count, 1.0, 0.0)
    later()
    diff_ref[...] = diffuse_rows(modes_ref[...], face_ref)


def put_blocks(source_ref, target_ref, base):
    chip = lax.axis_index("col") // 2
    rows = source_ref.shape[0] // 4
    for j in range(4):
        spot = pl.multiple_of(base + ((chip ^ j) & 3) * rows, rows)
        target_ref[pl.ds(spot, rows), :] = source_ref[j * rows : (j + 1) * rows, :]


def give_kernel(
    fetched,
    pair_in_ref, stoich_in_ref, speed_in_ref, loss_in_ref,
    diff_ref, emis_ref, live_ref, coef_in_ref,
    tend_ref, rate_ref, top_ref,
    field_ref, *chem_sems,
):
    if fetched:
        *chem_sems, coef_ref = chem_sems
    *chem, sems = chem_sems
    ready = fetch((pair_in_ref, stoich_in_ref, speed_in_ref, loss_in_ref), chem, sems)
    base = half_start(tend_ref.shape[1], False)
    if fetched:
        put_blocks(coef_in_ref, coef_ref, 0)
    else:
        coef_ref = coef_in_ref
    react(
        diff_ref[...], base, 0 if fetched else base, coef_ref, emis_ref, live_ref,
        ready, *chem, field_ref, tend_ref, rate_ref, top_ref,
    )


def keep_kernel(
    fetched,
    pair_in_ref, stoich_in_ref, speed_in_ref, loss_in_ref,
    diff_ref, emis_ref, live_ref, *refs,
):
    if fetched:
        give_ref, keep_ref, tend_ref, rate_ref, top_ref, coef_ref, field_ref, *chem_sems = refs
    else:
        coef_ref, tend_ref, rate_ref, top_ref, field_ref, *chem_sems = refs
    *chem, sems = chem_sems
    ready = fetch((pair_in_ref, stoich_in_ref, speed_in_ref, loss_in_ref), chem, sems)
    half = tend_ref.shape[1]
    base = half_start(half, True)
    if fetched:
        put_blocks(give_ref, coef_ref, half_start(half, False))
        put_blocks(keep_ref, coef_ref, base)
    react(
        diff_ref[...], base, base, coef_ref, emis_ref, live_ref,
        ready, *chem, field_ref, tend_ref, rate_ref, top_ref,
    )


STEP = 0.1
RATE_STEP = 0.3
RIDGE_SHARE = 0.05

F32 = jnp.float32
BF16 = jnp.bfloat16

NN = (((1,), (0,)), ((), ()))
NT = (((1,), (1,)), ((), ()))
TN = (((0,), (0,)), ((), ()))


def mm(a, b, dims=NN):
    return lax.dot_general(a, b, dims, preferred_element_type=F32)


def split(x):
    high = x.astype(BF16)
    return high, (x - high.astype(F32)).astype(BF16)


def mm3(a, b, dims=NN):
    return mm(a[0], b[0], dims) + (mm(a[0], b[1], dims) + mm(a[1], b[0], dims))


def diffuse_rows(modes, face_ref):
    faces = []
    for c in range(face_ref.shape[0] // LEV):
        faces += [face_ref[c * LEV : (c + 1) * LEV, :]] * S
    face = jnp.concatenate(faces, axis=0)
    rows = modes.shape[0]
    flux = face * (pltpu.roll(modes, rows - 1, 0) - modes)
    return modes + flux - pltpu.roll(flux, 1, 0)


def fetch(sources, targets, sems):
    copies = [
        pltpu.make_async_copy(source, target, sems.at[i])
        for i, (source, target) in enumerate(zip(sources, targets, strict=True))
    ]
    for copy in copies:
        copy.start()

    def wait():
        for copy in copies:
            copy.wait()

    return wait


def react(
    diffused, base, coef_base, coef_ref, emis_ref, live_ref, ready, pair_ref, stoich_ref, speed_ref, loss_ref,
    field_ref, tend_ref, rate_ref, top_ref,
):
    mode_bf = diffused.astype(BF16)
    members = tend_ref.shape[1]
    block = field_ref.shape[1]
    columns = diffused.shape[0] // (S * LEV)
    step = 16
    steps = LEV // step
    largest = jnp.full((1, R), 2.0**-120, F32)
    for b in range(members // block):
        lanes = slice(b * block, (b + 1) * block)
        spot = pl.ds(pl.multiple_of(base + b * block, block), block)
        member = pl.ds(pl.multiple_of(coef_base + b * block, block), block)
        field_ref[...] = mm(mode_bf, coef_ref[member, :], NT) * (1.0 / math.sqrt(R))
        if b == 0:
            ready()

        def part(i, _):
            c = i // steps
            low = (i - c * steps) * step
            first = c * (S * LEV) + low
            level = lax.broadcasted_iota(jnp.int32, (step, block), 0) + low
            profile = jnp.exp(level.astype(F32) * (-4.0 / LEV))
            live = live_ref[pl.ds(pl.multiple_of(c * LEV + low, step), step), 0:block] > 0.5

            def amount(s):
                return field_ref[pl.ds(pl.multiple_of(first + s * LEV, step), step), :]

            total = []
            for s in range(S):
                total.append(emis_ref[s : s + 1, spot] * profile - loss_ref[0, s] * amount(s))
            for r in range(NREAC):
                speed = speed_ref[0, r] * amount(pair_ref[0, r]) * amount(pair_ref[1, r])
                for s in range(S):
                    total[s] = total[s] + stoich_ref[s, r].astype(F32) * speed
            for s in range(S):
                tend_ref[pl.ds(pl.multiple_of(first + s * LEV, step), step), lanes] = jnp.where(
                    live, total[s], 0.0
                ).astype(BF16)
            return 0

        lax.fori_loop(0, columns * steps, part, 0, unroll=members <= block)
        rate = mm(tend_ref[:, lanes], mode_bf, TN)
        rate_ref[lanes, :] = rate
        largest = jnp.maximum(largest, jnp.max(jnp.abs(rate), axis=0, keepdims=True))
    power = jnp.maximum(jnp.floor(jnp.log(largest) * (1.0 / math.log(2.0))) + 2.0, -100.0)
    top_ref[...] = jnp.broadcast_to(power, top_ref.shape)


def half_start(members, keep):
    side = lax.axis_index("col") & 1
    return (side if keep else 1 - side) * members


def stage_kernel(
    columns,
    pair_hbm, stoich_hbm, speed_hbm, loss_hbm, table_hbm, level_face_hbm, idx_hbm, modes_hbm,
    counts_ref,
    pair_ref, stoich_ref, speed_ref, loss_ref, diff_ref, emis_ref, face_ref, live_ref,
    table_ref, level_face_ref, idx_ref, modes_ref, sems,
):
    later = fetch(
        (pair_hbm, stoich_hbm, speed_hbm, loss_hbm, modes_hbm),
        (pair_ref, stoich_ref, speed_ref, loss_ref, modes_ref),
        sems,
    )
    fetch(
        (table_hbm, level_face_hbm, idx_hbm), (table_ref, level_face_ref, idx_ref), sems.at[5:8]
    )()
    index = idx_ref[...]
    for s in range(S):
        row = jnp.zeros(index.shape, F32)
        for k in range(NEMIS):
            row = jnp.where(index == k, table_ref[s, k], row)
        emis_ref[s : s + 1, :] = row
    down = lax.broadcasted_iota(jnp.int32, (LEV, LEV), 0)
    across = lax.broadcasted_iota(jnp.int32, (LEV, LEV), 1)
    level = lax.broadcasted_iota(jnp.int32, (LEV, R), 0)
    for c in range(columns):
        part = slice(c * LEV, (c + 1) * LEV)
        count = counts_ref[:, c : c + 1]
        inner = (down == across) & (down + 1 < count)
        face = jnp.sum(jnp.where(inner, level_face_ref[c : c + 1, :], 0.0), axis=1, keepdims=True)
        face_ref[part, :] = jnp.broadcast_to(face, (LEV, R))
        live_ref[part, :] = jnp.where(level < count, 1.0, 0.0)
    later()
    diff_ref[...] = diffuse_rows(modes_ref[...], face_ref)


def first_kernel(plan, *allrefs):
    chem_in, chem, sems = allrefs[:4], allrefs[-5:-1], allrefs[-1]
    diff_ref, emis_ref, live_ref, *refs, field_ref = allrefs[4:-5]
    ready = fetch(chem_in, chem, sems)
    if plan:
        chip_ref, mine_ref, theirs_ref, tend_ref, rate_ref, top_ref, coef_ref = refs
        rows = chip_ref.shape[0]
        place = lax.axis_index("col")
        chip, side = place // 2, place % 2
        for j, pair in enumerate(plan):
            for ref, mask in (
                (mine_ref, jnp.where(side == 0, pair[0], pair[1])),
                (theirs_ref, jnp.where(side == 0, pair[1], pair[0])),
            ):
                spot = pl.multiple_of((chip ^ mask) * rows, rows)
                coef_ref[pl.ds(spot, rows), :] = ref[j * rows : (j + 1) * rows, :]
        coef_ref[pl.ds(pl.multiple_of(chip * rows, rows), rows), :] = chip_ref[...]
    else:
        coef_ref, tend_ref, rate_ref, top_ref = refs
    react(
        diff_ref[...], half_start(tend_ref.shape[1], False), coef_ref, emis_ref, live_ref,
        ready, *chem, field_ref, tend_ref, rate_ref, top_ref,
    )


def second_kernel(
    pair_in_ref, stoich_in_ref, speed_in_ref, loss_in_ref,
    diff_ref, emis_ref, live_ref, coef_ref,
    tend_ref, rate_ref, top_ref,
    field_ref, *chem_sems,
):
    *chem, sems = chem_sems
    ready = fetch((pair_in_ref, stoich_in_ref, speed_in_ref, loss_in_ref), chem, sems)
    react(
        diff_ref[...], half_start(tend_ref.shape[1], True), coef_ref, emis_ref, live_ref,
        ready, *chem, field_ref, tend_ref, rate_ref, top_ref,
    )


STEP = TIME_STEP * math.sqrt(R)


def ready_kernel(
    diff_ref, pull_ref, solve_ref, base_ref, diff_high_ref, diff_low_ref, high_ref, low_ref
):
    diffused = diff_ref[...]
    base_ref[...] = diffused + STEP * pull_ref[...]
    diff_high_ref[...], diff_low_ref[...] = split(diffused)
    high_ref[...], low_ref[...] = split(solve_ref[...])


def advance(base_ref, diff_high_ref, diff_low_ref, high_ref, low_ref, rate):
    transfer = mm3(split(rate), (high_ref[...], low_ref[...]), TN)
    moved = mm3((diff_high_ref[...], diff_low_ref[...]), split(transfer))
    return base_ref[...] - STEP * moved


def middle_kernel(
    total_rows,
    pair_in_ref, stoich_in_ref, speed_in_ref, loss_in_ref,
    base_ref, diff_high_ref, diff_low_ref, high_ref, low_ref,
    sum_ref, coef_ref, face_ref, emis_ref, live_ref,
    diff_ref, tend_ref, rate_ref, top_ref, coef_out_ref,
    field_ref, *chem_sems,
):
    *chem, sems = chem_sems
    ready = fetch((pair_in_ref, stoich_in_ref, speed_in_ref, loss_in_ref), chem, sems)
    raw = sum_ref[...]
    coef_out_ref[...] = (
        coef_ref[...].astype(F32) + RATE_STEP * (raw * (math.sqrt(R) / total_rows))
    ).astype(BF16)
    modes = advance(
        base_ref, diff_high_ref, diff_low_ref, high_ref, low_ref, raw * (1.0 / total_rows)
    )
    diffused = diffuse_rows(modes, face_ref)
    diff_ref[...] = diffused
    base = half_start(tend_ref.shape[1], False)
    react(
        diffused, base, base, coef_out_ref, emis_ref, live_ref,
        ready, *chem, field_ref, tend_ref, rate_ref, top_ref,
    )


def last_kernel(
    total_rows,
    base_ref, diff_high_ref, diff_low_ref, high_ref, low_ref,
    sum_ref, coef_ref,
    modes_ref, coef_out_ref,
):
    mine = coef_out_ref.shape[0]
    own = pl.ds(pl.multiple_of(lax.axis_index("col") * mine, mine), mine)
    coef_out_ref[...] = (
        coef_ref[own, :].astype(F32)
        + RATE_STEP * (sum_ref[own, :] * (math.sqrt(R) / total_rows))
    ).astype(BF16)
    modes_ref[...] = advance(
        base_ref, diff_high_ref, diff_low_ref, high_ref, low_ref,
        sum_ref[...] * (1.0 / total_rows),
    )


def identity():
    return (
        lax.broadcasted_iota(jnp.int32, (R, R), 0) == lax.broadcasted_iota(jnp.int32, (R, R), 1)
    ).astype(F32)


def refine(eye, high_ref, low_ref, inv_ref, gap):
    square = gap * gap
    factor = 2.0 / (2.0 - square)
    inv = inv_ref[...]
    halves = split(inv)
    rest = eye - mm3((high_ref[...], low_ref[...]), halves)
    inv_ref[...] = factor * (inv + mm3(halves, split(rest)))
    return square / (2.0 - square)


def inverse_start(ridge, steps, coef_ref, high_ref, low_ref, inv_ref, gap_ref):
    coef = coef_ref[...]
    eye = identity()
    gram = mm(coef, coef, TN) + ridge * eye
    top = jnp.max(jnp.sum(jnp.abs(gram), axis=0, keepdims=True))
    high_ref[...], low_ref[...] = split(gram)
    scale = 2.0 / (top + ridge)
    gap = (top - ridge) / (top + ridge)
    square = gap * gap
    factor = 2.0 / (2.0 - square)
    inv_ref[...] = (factor * scale) * (2.0 * eye - scale * gram)
    gap = lax.fori_loop(
        0, steps, lambda i, gap: refine(eye, high_ref, low_ref, inv_ref, gap),
        square / (2.0 - square),
    )
    gap_ref[...] = jnp.full(gap_ref.shape, gap, F32)


def inverse_end(
    gap_in_ref, high_ref, low_ref, inv_in_ref, coef_ref, give_ref, keep_ref,
    solve_ref, pull_ref, inv_ref,
):
    eye = identity()
    inv_ref[...] = inv_in_ref[...]
    lax.while_loop(
        lambda gap: gap > 1e-5,
        lambda gap: refine(eye, high_ref, low_ref, inv_ref, gap),
        jnp.max(gap_in_ref[...]),
    )
    coef = coef_ref[...]
    high, low = split(inv_ref[...])
    solve = mm(coef, high) + mm(coef, low)
    solve_ref[...] = solve
    half = give_ref.shape[1]
    parts = []
    for ref, keep in ((give_ref, False), (keep_ref, True)):
        start = pl.multiple_of(half_start(half, keep), half)
        high, low = split(solve_ref[pl.ds(start, half), :])
        parts.append(mm(ref[...], high) + mm(ref[...], low))
    pull_ref[...] = parts[0] + parts[1]


VMEM_LIMIT = 48 * 1024 * 1024


def call(kernel, n_hbm, outs, scratch, *args):
    args = [
        pltpu.with_memory_space_constraint(arg, pltpu.HBM) if i < n_hbm else arg
        for i, arg in enumerate(args)
    ]
    return pl.pallas_call(
        kernel,
        in_specs=[
            pl.BlockSpec(memory_space=pltpu.HBM if i < n_hbm else pltpu.VMEM)
            for i in range(len(args))
        ],
        out_specs=[pl.BlockSpec(memory_space=pltpu.VMEM)] * len(outs),
        out_shape=[jax.ShapeDtypeStruct(shape, dtype) for shape, dtype in outs],
        scratch_shapes=scratch,
        compiler_params=pltpu.CompilerParams(vmem_limit_bytes=VMEM_LIMIT),
    )(*args)


def tied(value, first):
    return lax.optimization_barrier((first, value))[1]


def swap(value, n, masks):
    return lax.ppermute(value, "col", [(i, i ^ masks[i % 2]) for i in range(n) if masks[i % 2]])


def fetch_half(chip_rows, n):
    blocks = []
    for j in range(4):
        pairs = []
        for target in range(n):
            chip, side = target // 2, target % 2
            if chip // 4 == 1 - side:
                if j:
                    pairs.append(((chip ^ j) * 2 + side, target))
            else:
                pairs.append(((chip ^ j ^ 4) * 2 + 1 - side, target))
        blocks.append(lax.ppermute(chip_rows, "col", pairs))
    place = lax.axis_index("col")
    blocks[0] = jnp.where(place // 8 == 1 - place % 2, chip_rows, blocks[0])
    return blocks


EXTRA = 8
LIFT = 15.0


def encode(part, power):
    scaled = (part * jnp.exp2(LIFT - power)).astype(jnp.float16)
    powers = jnp.broadcast_to(power, (EXTRA, R)).astype(jnp.float16)
    return lax.optimization_barrier(jnp.concatenate([scaled, powers], 0))


def decode(message):
    rows = message.shape[0] - EXTRA
    power = message[rows : rows + 1].astype(F32)
    return message[:rows].astype(F32) * jnp.exp2(power - LIFT), power


def sum_over(give, top, keep_half, n, work, prepare):
    got = swap(jnp.concatenate([give, top], 0), n, (1, 1))
    keep, keep_top, state = keep_half()
    got, keep = lax.optimization_barrier((got, keep))
    half = give.shape[0]
    side = lax.axis_index("col") & 1
    part = keep + got[:half]
    power = jnp.maximum(keep_top[:1], got[half : half + 1]) + 1.0
    work = list(work)
    mask = 2
    while mask < n:
        masks = [mask, mask * 2, mask * 3] if mask * 2 < n else [mask]
        message = encode(part, power)
        others = [swap(message, n, (m, m)) for m in masks]
        mask *= 4 if len(masks) == 3 else 2
        while work:
            state = work.pop(0)(state, message)
            others, state = lax.optimization_barrier((others, state))
            if mask < n:
                break
        part, power = decode(message)
        for other in others:
            more, high = decode(other)
            part = part + more
            power = jnp.maximum(power, high)
        power = power + float(len(masks))
    other = swap(part, n, (1, 1))
    state = prepare(state, part)
    other, state = lax.optimization_barrier((other, state))
    total = jnp.where(
        side == 0, jnp.concatenate([part, other], 0), jnp.concatenate([other, part], 0)
    )
    return total, state


def on_device(
    mode_rows,
    coeffs,
    diffusivity,
    counts,
    emis_idx,
    emis_table,
    reactants,
    stoich,
    rate_consts,
    loss_rates,
):
    n = lax.axis_size("col")
    rows = mode_rows.shape[0]
    total_rows = rows * n
    mine = coeffs.shape[0]
    members = mine * n
    columns = counts.shape[0]
    ridge = RIDGE_SHARE * members
    half = members // 2
    block = math.gcd(half, 256)
    rows_f32 = ((rows, R), F32)
    rows_bf = ((rows, R), BF16)
    tend_out = ((rows, half), BF16)
    half_out = ((half, R), F32)
    rate_out = ((members, R), F32)
    top_out = ((EXTRA, R), F32)
    coef_out = ((members, R), BF16)
    tables = (reactants.T, stoich.T, rate_consts.reshape(1, NREAC), loss_rates.reshape(1, S))
    react_tmp = [
        pltpu.VMEM((rows, block), F32),
        *(pltpu.SMEM(value.shape, value.dtype) for value in tables),
        pltpu.SemaphoreType.DMA((len(tables),)),
    ]
    square = ((R, R), F32)
    square_bf = ((R, R), BF16)

    def stage(modes):
        by_level = ((columns * LEV, R), F32)
        index = emis_idx.reshape(1, members)
        *chem, diff, emis, face, live = call(
            functools.partial(stage_kernel, columns), 8,
            [(value.shape, value.dtype) for value in tables]
            + [rows_f32, ((S, members), F32), by_level, by_level],
            [
                pltpu.SMEM((S, NEMIS), F32),
                pltpu.VMEM(diffusivity.shape, F32),
                pltpu.VMEM((1, members), jnp.int32),
                pltpu.VMEM((rows, R), F32),
                pltpu.SemaphoreType.DMA((8,)),
            ],
            *tables, emis_table.T, diffusivity, index, modes, counts.reshape(1, columns),
        )
        return chem, diff, emis, face, live

    if n == 16:
        other = swap(coeffs, n, (1, 1))
        side = lax.axis_index("col") & 1
        chip = jnp.where(
            side == 0, jnp.concatenate([coeffs, other], 0), jnp.concatenate([other, coeffs], 0)
        )
        blocks = fetch_half(chip, n)
        chem, diff, emis, face, live = stage(tied(mode_rows, chip))
        blocks, diff = lax.optimization_barrier((blocks, diff))
        coef = jnp.concatenate(blocks, 0)
    else:
        coef = lax.all_to_all(jnp.tile(coeffs, (n, 1)), "col", 0, 0, tiled=True)
        chem, diff, emis, face, live = stage(mode_rows)
    fetched = n == 16
    keep_coef = swap(coef, n, (1, 1)) if fetched else None
    tend, rate, top = call(
        functools.partial(give_kernel, fetched), 0,
        [tend_out, half_out, top_out],
        react_tmp + [pltpu.VMEM((half, R), BF16)] * fetched,
        *chem, diff, emis, live, coef,
    )
    if fetched:
        keep_coef, rate = lax.optimization_barrier((keep_coef, rate))

    def summed(rate, top, coef, tend, diff, keep_coef=None):
        def keep_half():
            fetched = keep_coef is not None
            tend_keep, keep, keep_top, *made = call(
                functools.partial(keep_kernel, fetched), 0,
                [tend_out, half_out, top_out] + [coef_out] * fetched, react_tmp,
                *chem, tied(diff, rate), emis, live, coef, *([keep_coef] if fetched else []),
            )
            return keep, keep_top, (tend_keep, made[0] if fetched else coef)

        def start(state, ready):
            coef = state[1]
            return state, call(
                functools.partial(inverse_start, ridge, 4), 0,
                [square_bf, square_bf, square, top_out], [], tied(coef, ready),
            )

        def end(state, ready):
            (tend_keep, coef), (high, low, inv, gap) = tied(state, ready)
            return coef, *call(
                inverse_end, 0, [rate_out, rows_f32], [pltpu.VMEM((R, R), F32)],
                gap, high, low, inv, coef, tend, tend_keep,
            )

        def prepare(state, ready):
            coef, solved, pull = tied(state, ready)
            return coef, call(
                ready_kernel, 0,
                [rows_f32, rows_bf, rows_bf, ((members, R), BF16), ((members, R), BF16)], [],
                diff, pull, solved,
            )

        return sum_over(rate, top, keep_half, n, (start, end), prepare)

    for _ in range(NSUB - 1):
        total, (coef, prepared) = summed(rate, top, coef, tend, diff, keep_coef)
        keep_coef = None
        diff, tend, rate, top, coef = call(
            functools.partial(middle_kernel, total_rows), 0,
            [rows_f32, tend_out, half_out, top_out, coef_out], react_tmp,
            *chem, *prepared, total, coef, face, emis, live,
        )
    total, (coef, prepared) = summed(rate, top, coef, tend, diff, keep_coef)
    return tuple(
        call(
            functools.partial(last_kernel, total_rows), 0,
            [rows_f32, ((mine, R), BF16)], [],
            *prepared, total, coef,
        )
    )


def solution(mesh):
    placed = (
        P(("grp", "col"), None),
        P(("grp", "col"), None),
        P(("grp", "col"), None),
        P(("grp", "col")),
        P("grp"),
        P(),
        P(),
        P(),
        P(),
        P(),
    )
    return jax.shard_map(
        on_device,
        mesh=mesh,
        in_specs=placed,
        out_specs=(P(("grp", "col"), None), P(("grp", "col"), None)),
        check_vma=False,
    )
```

```python
import functools
import math

import jax
import jax.numpy as jnp
from jax import lax
from jax.experimental import pallas as pl
from jax.experimental.pallas import tpu as pltpu
from jax.sharding import PartitionSpec as P

S = 8
LEV = 64
R = 256
NREAC = 12
NEMIS = 16
NSUB = 2

TIME_STEP = 0.1
RATE_STEP = 0.3
RIDGE_SHARE = 0.05

F32 = jnp.float32
BF16 = jnp.bfloat16

NN = (((1,), (0,)), ((), ()))
NT = (((1,), (1,)), ((), ()))
TN = (((0,), (0,)), ((), ()))


def mm(a, b, dims=NN):
    return lax.dot_general(a, b, dims, preferred_element_type=F32)


def split(x):
    high = x.astype(BF16)
    return high, (x - high.astype(F32)).astype(BF16)


def mm3(a, b, dims=NN):
    return mm(a[0], b[0], dims) + (mm(a[0], b[1], dims) + mm(a[1], b[0], dims))


def diffuse_rows(modes, face_ref):
    faces = []
    for c in range(face_ref.shape[0] // LEV):
        faces += [face_ref[c * LEV : (c + 1) * LEV, :]] * S
    face = jnp.concatenate(faces, axis=0)
    rows = modes.shape[0]
    flux = face * (pltpu.roll(modes, rows - 1, 0) - modes)
    return modes + flux - pltpu.roll(flux, 1, 0)


def fetch(sources, targets, sems):
    copies = [
        pltpu.make_async_copy(source, target, sems.at[i])
        for i, (source, target) in enumerate(zip(sources, targets, strict=True))
    ]
    for copy in copies:
        copy.start()

    def wait():
        for copy in copies:
            copy.wait()

    return wait


def react(
    diffused, base, coef_ref, emis_ref, live_ref, ready, pair_ref, stoich_ref, speed_ref, loss_ref,
    field_ref, tend_ref, rate_ref, top_ref,
):
    mode_bf = diffused.astype(BF16)
    members = tend_ref.shape[1]
    block = field_ref.shape[1]
    columns = diffused.shape[0] // (S * LEV)
    step = 16
    steps = LEV // step
    largest = jnp.full((1, R), 2.0**-120, F32)
    for b in range(members // block):
        lanes = slice(b * block, (b + 1) * block)
        spot = pl.ds(pl.multiple_of(base + b * block, block), block)
        field_ref[...] = mm(mode_bf, coef_ref[spot, :], NT) * (1.0 / math.sqrt(R))
        if b == 0:
            ready()

        def part(i, _):
            c = i // steps
            low = (i - c * steps) * step
            first = c * (S * LEV) + low
            level = lax.broadcasted_iota(jnp.int32, (step, block), 0) + low
            profile = jnp.exp(level.astype(F32) * (-4.0 / LEV))
            live = live_ref[pl.ds(pl.multiple_of(c * LEV + low, step), step), 0:block] > 0.5

            def amount(s):
                return field_ref[pl.ds(pl.multiple_of(first + s * LEV, step), step), :]

            total = []
            for s in range(S):
                total.append(emis_ref[s : s + 1, spot] * profile - loss_ref[0, s] * amount(s))
            for r in range(NREAC):
                speed = speed_ref[0, r] * amount(pair_ref[0, r]) * amount(pair_ref[1, r])
                for s in range(S):
                    total[s] = total[s] + stoich_ref[s, r].astype(F32) * speed
            for s in range(S):
                tend_ref[pl.ds(pl.multiple_of(first + s * LEV, step), step), lanes] = jnp.where(
                    live, total[s], 0.0
                ).astype(BF16)
            return 0

        lax.fori_loop(0, columns * steps, part, 0, unroll=members <= block)
        rate = mm(tend_ref[:, lanes], mode_bf, TN)
        rate_ref[lanes, :] = rate
        largest = jnp.maximum(largest, jnp.max(jnp.abs(rate), axis=0, keepdims=True))
    power = jnp.maximum(jnp.floor(jnp.log(largest) * (1.0 / math.log(2.0))) + 2.0, -100.0)
    top_ref[...] = jnp.broadcast_to(power, top_ref.shape)


def half_start(members, keep):
    side = lax.axis_index("col") & 1
    return (side if keep else 1 - side) * members


def stage_kernel(
    columns,
    pair_hbm, stoich_hbm, speed_hbm, loss_hbm, table_hbm, level_face_hbm, idx_hbm, modes_hbm,
    counts_ref,
    pair_ref, stoich_ref, speed_ref, loss_ref, diff_ref, emis_ref, face_ref, live_ref,
    table_ref, level_face_ref, idx_ref, modes_ref, sems,
):
    later = fetch(
        (pair_hbm, stoich_hbm, speed_hbm, loss_hbm, modes_hbm),
        (pair_ref, stoich_ref, speed_ref, loss_ref, modes_ref),
        sems,
    )
    fetch(
        (table_hbm, level_face_hbm, idx_hbm), (table_ref, level_face_ref, idx_ref), sems.at[5:8]
    )()
    index = idx_ref[...]
    for s in range(S):
        row = jnp.zeros(index.shape, F32)
        for k in range(NEMIS):
            row = jnp.where(index == k, table_ref[s, k], row)
        emis_ref[s : s + 1, :] = row
    down = lax.broadcasted_iota(jnp.int32, (LEV, LEV), 0)
    across = lax.broadcasted_iota(jnp.int32, (LEV, LEV), 1)
    level = lax.broadcasted_iota(jnp.int32, (LEV, R), 0)
    for c in range(columns):
        part = slice(c * LEV, (c + 1) * LEV)
        count = counts_ref[:, c : c + 1]
        inner = (down == across) & (down + 1 < count)
        face = jnp.sum(jnp.where(inner, level_face_ref[c : c + 1, :], 0.0), axis=1, keepdims=True)
        face_ref[part, :] = jnp.broadcast_to(face, (LEV, R))
        live_ref[part, :] = jnp.where(level < count, 1.0, 0.0)
    later()
    diff_ref[...] = diffuse_rows(modes_ref[...], face_ref)


def first_kernel(plan, *allrefs):
    chem_in, chem, sems = allrefs[:4], allrefs[-5:-1], allrefs[-1]
    diff_ref, emis_ref, live_ref, *refs, field_ref = allrefs[4:-5]
    ready = fetch(chem_in, chem, sems)
    if plan:
        chip_ref, mine_ref, theirs_ref, tend_ref, rate_ref, top_ref, coef_ref = refs
        rows = chip_ref.shape[0]
        place = lax.axis_index("col")
        chip, side = place // 2, place % 2
        for j, pair in enumerate(plan):
            for ref, mask in (
                (mine_ref, jnp.where(side == 0, pair[0], pair[1])),
                (theirs_ref, jnp.where(side == 0, pair[1], pair[0])),
            ):
                spot = pl.multiple_of((chip ^ mask) * rows, rows)
                coef_ref[pl.ds(spot, rows), :] = ref[j * rows : (j + 1) * rows, :]
        coef_ref[pl.ds(pl.multiple_of(chip * rows, rows), rows), :] = chip_ref[...]
    else:
        coef_ref, tend_ref, rate_ref, top_ref = refs
    react(
        diff_ref[...], half_start(tend_ref.shape[1], False), coef_ref, emis_ref, live_ref,
        ready, *chem, field_ref, tend_ref, rate_ref, top_ref,
    )


def second_kernel(
    pair_in_ref, stoich_in_ref, speed_in_ref, loss_in_ref,
    diff_ref, emis_ref, live_ref, coef_ref,
    tend_ref, rate_ref, top_ref,
    field_ref, *chem_sems,
):
    *chem, sems = chem_sems
    ready = fetch((pair_in_ref, stoich_in_ref, speed_in_ref, loss_in_ref), chem, sems)
    react(
        diff_ref[...], half_start(tend_ref.shape[1], True), coef_ref, emis_ref, live_ref,
        ready, *chem, field_ref, tend_ref, rate_ref, top_ref,
    )


STEP = TIME_STEP * math.sqrt(R)


def ready_kernel(
    diff_ref, pull_ref, solve_ref, base_ref, diff_high_ref, diff_low_ref, high_ref, low_ref
):
    diffused = diff_ref[...]
    base_ref[...] = diffused + STEP * pull_ref[...]
    diff_high_ref[...], diff_low_ref[...] = split(diffused)
    high_ref[...], low_ref[...] = split(solve_ref[...])


def advance(base_ref, diff_high_ref, diff_low_ref, high_ref, low_ref, rate):
    transfer = mm3(split(rate), (high_ref[...], low_ref[...]), TN)
    moved = mm3((diff_high_ref[...], diff_low_ref[...]), split(transfer))
    return base_ref[...] - STEP * moved


def middle_kernel(
    total_rows,
    pair_in_ref, stoich_in_ref, speed_in_ref, loss_in_ref,
    base_ref, diff_high_ref, diff_low_ref, high_ref, low_ref,
    sum_ref, coef_ref, face_ref, emis_ref, live_ref,
    diff_ref, tend_ref, rate_ref, top_ref, coef_out_ref,
    field_ref, *chem_sems,
):
    *chem, sems = chem_sems
    ready = fetch((pair_in_ref, stoich_in_ref, speed_in_ref, loss_in_ref), chem, sems)
    raw = sum_ref[...]
    coef_out_ref[...] = (
        coef_ref[...].astype(F32) + RATE_STEP * (raw * (math.sqrt(R) / total_rows))
    ).astype(BF16)
    modes = advance(
        base_ref, diff_high_ref, diff_low_ref, high_ref, low_ref, raw * (1.0 / total_rows)
    )
    diffused = diffuse_rows(modes, face_ref)
    diff_ref[...] = diffused
    react(
        diffused, half_start(tend_ref.shape[1], False), coef_out_ref, emis_ref, live_ref,
        ready, *chem, field_ref, tend_ref, rate_ref, top_ref,
    )


def last_kernel(
    total_rows,
    base_ref, diff_high_ref, diff_low_ref, high_ref, low_ref,
    sum_ref, coef_ref,
    modes_ref, coef_out_ref,
):
    mine = coef_out_ref.shape[0]
    own = pl.ds(pl.multiple_of(lax.axis_index("col") * mine, mine), mine)
    coef_out_ref[...] = (
        coef_ref[own, :].astype(F32)
        + RATE_STEP * (sum_ref[own, :] * (math.sqrt(R) / total_rows))
    ).astype(BF16)
    modes_ref[...] = advance(
        base_ref, diff_high_ref, diff_low_ref, high_ref, low_ref,
        sum_ref[...] * (1.0 / total_rows),
    )


def identity():
    return (
        lax.broadcasted_iota(jnp.int32, (R, R), 0) == lax.broadcasted_iota(jnp.int32, (R, R), 1)
    ).astype(F32)


def refine(eye, high_ref, low_ref, inv_ref, gap):
    square = gap * gap
    factor = 2.0 / (2.0 - square)
    inv = inv_ref[...]
    halves = split(inv)
    rest = eye - mm3((high_ref[...], low_ref[...]), halves)
    inv_ref[...] = factor * (inv + mm3(halves, split(rest)))
    return square / (2.0 - square)


def inverse_start(ridge, steps, coef_ref, high_ref, low_ref, inv_ref, gap_ref):
    coef = coef_ref[...]
    eye = identity()
    gram = mm(coef, coef, TN) + ridge * eye
    top = jnp.max(jnp.sum(jnp.abs(gram), axis=0, keepdims=True))
    high_ref[...], low_ref[...] = split(gram)
    scale = 2.0 / (top + ridge)
    gap = (top - ridge) / (top + ridge)
    square = gap * gap
    factor = 2.0 / (2.0 - square)
    inv_ref[...] = (factor * scale) * (2.0 * eye - scale * gram)
    gap = lax.fori_loop(
        0, steps, lambda i, gap: refine(eye, high_ref, low_ref, inv_ref, gap),
        square / (2.0 - square),
    )
    gap_ref[...] = jnp.full(gap_ref.shape, gap, F32)


def inverse_end(
    gap_in_ref, high_ref, low_ref, inv_in_ref, coef_ref, give_ref, keep_ref,
    solve_ref, pull_ref, inv_ref,
):
    eye = identity()
    inv_ref[...] = inv_in_ref[...]
    lax.while_loop(
        lambda gap: gap > 1e-5,
        lambda gap: refine(eye, high_ref, low_ref, inv_ref, gap),
        jnp.max(gap_in_ref[...]),
    )
    coef = coef_ref[...]
    high, low = split(inv_ref[...])
    solve = mm(coef, high) + mm(coef, low)
    solve_ref[...] = solve
    half = give_ref.shape[1]
    parts = []
    for ref, keep in ((give_ref, False), (keep_ref, True)):
        start = pl.multiple_of(half_start(half, keep), half)
        high, low = split(solve_ref[pl.ds(start, half), :])
        parts.append(mm(ref[...], high) + mm(ref[...], low))
    pull_ref[...] = parts[0] + parts[1]


VMEM_LIMIT = 48 * 1024 * 1024


def call(kernel, n_hbm, outs, scratch, *args):
    args = [
        pltpu.with_memory_space_constraint(arg, pltpu.HBM) if i < n_hbm else arg
        for i, arg in enumerate(args)
    ]
    return pl.pallas_call(
        kernel,
        in_specs=[
            pl.BlockSpec(memory_space=pltpu.HBM if i < n_hbm else pltpu.VMEM)
            for i in range(len(args))
        ],
        out_specs=[pl.BlockSpec(memory_space=pltpu.VMEM)] * len(outs),
        out_shape=[jax.ShapeDtypeStruct(shape, dtype) for shape, dtype in outs],
        scratch_shapes=scratch,
        compiler_params=pltpu.CompilerParams(vmem_limit_bytes=VMEM_LIMIT),
    )(*args)


def tied(value, first):
    return lax.optimization_barrier((first, value))[1]


def swap(value, n, masks):
    return lax.ppermute(value, "col", [(i, i ^ masks[i % 2]) for i in range(n) if masks[i % 2]])


EXTRA = 8
LIFT = 15.0


def encode(part, power):
    scaled = (part * jnp.exp2(LIFT - power)).astype(jnp.float16)
    powers = jnp.broadcast_to(power, (EXTRA, R)).astype(jnp.float16)
    return lax.optimization_barrier(jnp.concatenate([scaled, powers], 0))


def decode(message):
    rows = message.shape[0] - EXTRA
    power = message[rows : rows + 1].astype(F32)
    return message[:rows].astype(F32) * jnp.exp2(power - LIFT), power


def sum_over(give, top, keep_half, n, work, prepare):
    got = swap(jnp.concatenate([give, top], 0), n, (1, 1))
    keep, keep_top, state = keep_half()
    got, keep = lax.optimization_barrier((got, keep))
    half = give.shape[0]
    side = lax.axis_index("col") & 1
    part = keep + got[:half]
    power = jnp.maximum(keep_top[:1], got[half : half + 1]) + 1.0
    work = list(work)
    mask = 2
    while mask < n:
        masks = [mask, mask * 2, mask * 3] if mask * 2 < n else [mask]
        message = encode(part, power)
        others = [swap(message, n, (m, m)) for m in masks]
        mask *= 4 if len(masks) == 3 else 2
        while work:
            state = work.pop(0)(state, message)
            others, state = lax.optimization_barrier((others, state))
            if mask < n:
                break
        part, power = decode(message)
        for other in others:
            more, high = decode(other)
            part = part + more
            power = jnp.maximum(power, high)
        power = power + float(len(masks))
    other = swap(part, n, (1, 1))
    state = prepare(state, part)
    other, state = lax.optimization_barrier((other, state))
    total = jnp.where(
        side == 0, jnp.concatenate([part, other], 0), jnp.concatenate([other, part], 0)
    )
    return total, state


def on_device(
    mode_rows,
    coeffs,
    diffusivity,
    counts,
    emis_idx,
    emis_table,
    reactants,
    stoich,
    rate_consts,
    loss_rates,
):
    n = lax.axis_size("col")
    rows = mode_rows.shape[0]
    total_rows = rows * n
    mine = coeffs.shape[0]
    members = mine * n
    columns = counts.shape[0]
    ridge = RIDGE_SHARE * members
    half = members // 2
    block = math.gcd(half, 256)
    rows_f32 = ((rows, R), F32)
    rows_bf = ((rows, R), BF16)
    tend_out = ((rows, half), BF16)
    half_out = ((half, R), F32)
    rate_out = ((members, R), F32)
    top_out = ((EXTRA, R), F32)
    coef_out = ((members, R), BF16)
    tables = (reactants.T, stoich.T, rate_consts.reshape(1, NREAC), loss_rates.reshape(1, S))
    react_tmp = [
        pltpu.VMEM((rows, block), F32),
        *(pltpu.SMEM(value.shape, value.dtype) for value in tables),
        pltpu.SemaphoreType.DMA((len(tables),)),
    ]
    square = ((R, R), F32)
    square_bf = ((R, R), BF16)

    def stage(modes):
        by_level = ((columns * LEV, R), F32)
        index = emis_idx.reshape(1, members)
        *chem, diff, emis, face, live = call(
            functools.partial(stage_kernel, columns), 8,
            [(value.shape, value.dtype) for value in tables]
            + [rows_f32, ((S, members), F32), by_level, by_level],
            [
                pltpu.SMEM((S, NEMIS), F32),
                pltpu.VMEM(diffusivity.shape, F32),
                pltpu.VMEM((1, members), jnp.int32),
                pltpu.VMEM((rows, R), F32),
                pltpu.SemaphoreType.DMA((8,)),
            ],
            *tables, emis_table.T, diffusivity, index, modes, counts.reshape(1, columns),
        )
        return chem, diff, emis, face, live

    if n == 16:
        plan = ((1, 1), (2, 3), (4, 6), (5, 7))
        other = swap(coeffs, n, (1, 1))
        side = lax.axis_index("col") & 1
        chip = jnp.where(
            side == 0, jnp.concatenate([coeffs, other], 0), jnp.concatenate([other, coeffs], 0)
        )
        fetched = [swap(chip, n, (2 * a, 2 * b)) for a, b in plan]
        chem, diff, emis, face, live = stage(tied(mode_rows, chip))
        fetched, diff = lax.optimization_barrier((fetched, diff))
        mine_rows = jnp.concatenate(fetched, 0)
        theirs = swap(mine_rows, n, (1, 1))
        gathered = (chip, mine_rows, theirs)
        tend, rate, top, coef = call(
            functools.partial(first_kernel, plan), 0,
            [tend_out, half_out, top_out, coef_out], react_tmp,
            *chem, diff, emis, live, *gathered,
        )
    else:
        coef = lax.all_to_all(jnp.tile(coeffs, (n, 1)), "col", 0, 0, tiled=True)
        chem, diff, emis, face, live = stage(mode_rows)
        tend, rate, top = call(
            functools.partial(first_kernel, ()), 0,
            [tend_out, half_out, top_out], react_tmp,
            *chem, diff, emis, live, coef,
        )

    def summed(rate, top, coef, tend, diff):
        def keep_half():
            tend_keep, keep, keep_top = call(
                second_kernel, 0, [tend_out, half_out, top_out], react_tmp,
                *chem, tied(diff, rate), emis, live, coef,
            )
            return keep, keep_top, tend_keep

        def start(tend_keep, ready):
            return tend_keep, call(
                functools.partial(inverse_start, ridge, 4), 0,
                [square_bf, square_bf, square, top_out], [], tied(coef, ready),
            )

        def end(state, ready):
            tend_keep, (high, low, inv, gap) = tied(state, ready)
            return call(
                inverse_end, 0, [rate_out, rows_f32], [pltpu.VMEM((R, R), F32)],
                gap, high, low, inv, coef, tend, tend_keep,
            )

        def prepare(state, ready):
            solved, pull = tied(state, ready)
            return call(
                ready_kernel, 0,
                [rows_f32, rows_bf, rows_bf, ((members, R), BF16), ((members, R), BF16)], [],
                diff, pull, solved,
            )

        return sum_over(rate, top, keep_half, n, (start, end), prepare)

    for _ in range(NSUB - 1):
        total, prepared = summed(rate, top, coef, tend, diff)
        diff, tend, rate, top, coef = call(
            functools.partial(middle_kernel, total_rows), 0,
            [rows_f32, tend_out, half_out, top_out, coef_out], react_tmp,
            *chem, *prepared, total, coef, face, emis, live,
        )
    total, prepared = summed(rate, top, coef, tend, diff)
    return tuple(
        call(
            functools.partial(last_kernel, total_rows), 0,
            [rows_f32, ((mine, R), BF16)], [],
            *prepared, total, coef,
        )
    )


def solution(mesh):
    placed = (
        P(("grp", "col"), None),
        P(("grp", "col"), None),
        P(("grp", "col"), None),
        P(("grp", "col")),
        P("grp"),
        P(),
        P(),
        P(),
        P(),
        P(),
    )
    return jax.shard_map(
        on_device,
        mesh=mesh,
        in_specs=placed,
        out_specs=(P(("grp", "col"), None), P(("grp", "col"), None)),
        check_vma=False,
    )
```

```python
import functools
import math

import jax
import jax.numpy as jnp
from jax import lax
from jax.experimental import pallas as pl
from jax.experimental.pallas import tpu as pltpu
from jax.sharding import PartitionSpec as P

S = 8
LEV = 64
R = 256
NREAC = 12
NEMIS = 16
NSUB = 2

TIME_STEP = 0.1
RATE_STEP = 0.3
RIDGE_SHARE = 0.05

F32 = jnp.float32
BF16 = jnp.bfloat16

NN = (((1,), (0,)), ((), ()))
NT = (((1,), (1,)), ((), ()))
TN = (((0,), (0,)), ((), ()))


def mm(a, b, dims=NN):
    return lax.dot_general(a, b, dims, preferred_element_type=F32)


def split(x):
    high = x.astype(BF16)
    return high, (x - high.astype(F32)).astype(BF16)


def mm3(a, b, dims=NN):
    return mm(a[0], b[0], dims) + (mm(a[0], b[1], dims) + mm(a[1], b[0], dims))


def diffuse_rows(modes, face_ref):
    faces = []
    for c in range(face_ref.shape[0] // LEV):
        faces += [face_ref[c * LEV : (c + 1) * LEV, :]] * S
    face = jnp.concatenate(faces, axis=0)
    rows = modes.shape[0]
    flux = face * (pltpu.roll(modes, rows - 1, 0) - modes)
    return modes + flux - pltpu.roll(flux, 1, 0)


def fetch(sources, targets, sems):
    copies = [
        pltpu.make_async_copy(source, target, sems.at[i])
        for i, (source, target) in enumerate(zip(sources, targets, strict=True))
    ]
    for copy in copies:
        copy.start()

    def wait():
        for copy in copies:
            copy.wait()

    return wait


def react(
    diffused, base, coef_ref, emis_ref, live_ref, ready, pair_ref, stoich_ref, speed_ref, loss_ref,
    field_ref, tend_ref, rate_ref, top_ref,
):
    mode_bf = diffused.astype(BF16)
    members = tend_ref.shape[1]
    block = field_ref.shape[1]
    columns = diffused.shape[0] // (S * LEV)
    step = 16
    steps = LEV // step
    largest = jnp.full((1, R), 2.0**-120, F32)
    for b in range(members // block):
        lanes = slice(b * block, (b + 1) * block)
        spot = pl.ds(pl.multiple_of(base + b * block, block), block)
        field_ref[...] = mm(mode_bf, coef_ref[spot, :], NT) * (1.0 / math.sqrt(R))
        if b == 0:
            ready()

        def part(i, _):
            c = i // steps
            low = (i - c * steps) * step
            first = c * (S * LEV) + low
            level = lax.broadcasted_iota(jnp.int32, (step, block), 0) + low
            profile = jnp.exp(level.astype(F32) * (-4.0 / LEV))
            live = live_ref[pl.ds(pl.multiple_of(c * LEV + low, step), step), 0:block] > 0.5

            def amount(s):
                return field_ref[pl.ds(pl.multiple_of(first + s * LEV, step), step), :]

            total = []
            for s in range(S):
                total.append(emis_ref[s : s + 1, spot] * profile - loss_ref[0, s] * amount(s))
            for r in range(NREAC):
                speed = speed_ref[0, r] * amount(pair_ref[0, r]) * amount(pair_ref[1, r])
                for s in range(S):
                    total[s] = total[s] + stoich_ref[s, r].astype(F32) * speed
            for s in range(S):
                tend_ref[pl.ds(pl.multiple_of(first + s * LEV, step), step), lanes] = jnp.where(
                    live, total[s], 0.0
                ).astype(BF16)
            return 0

        lax.fori_loop(0, columns * steps, part, 0, unroll=members <= block)
        rate = mm(tend_ref[:, lanes], mode_bf, TN)
        rate_ref[lanes, :] = rate
        largest = jnp.maximum(largest, jnp.max(jnp.abs(rate), axis=0, keepdims=True))
    power = jnp.maximum(jnp.floor(jnp.log(largest) * (1.0 / math.log(2.0))) + 2.0, -100.0)
    top_ref[...] = jnp.broadcast_to(power, top_ref.shape)


def half_start(members, keep):
    side = lax.axis_index("col") & 1
    return (side if keep else 1 - side) * members


def stage_kernel(
    columns,
    pair_hbm, stoich_hbm, speed_hbm, loss_hbm, table_hbm, level_face_hbm, idx_hbm, modes_hbm,
    counts_ref,
    pair_ref, stoich_ref, speed_ref, loss_ref, diff_ref, emis_ref, face_ref, live_ref,
    table_ref, level_face_ref, idx_ref, modes_ref, sems,
):
    later = fetch(
        (pair_hbm, stoich_hbm, speed_hbm, loss_hbm, modes_hbm),
        (pair_ref, stoich_ref, speed_ref, loss_ref, modes_ref),
        sems,
    )
    fetch(
        (table_hbm, level_face_hbm, idx_hbm), (table_ref, level_face_ref, idx_ref), sems.at[5:8]
    )()
    index = idx_ref[...]
    for s in range(S):
        row = jnp.zeros(index.shape, F32)
        for k in range(NEMIS):
            row = jnp.where(index == k, table_ref[s, k], row)
        emis_ref[s : s + 1, :] = row
    down = lax.broadcasted_iota(jnp.int32, (LEV, LEV), 0)
    across = lax.broadcasted_iota(jnp.int32, (LEV, LEV), 1)
    level = lax.broadcasted_iota(jnp.int32, (LEV, R), 0)
    for c in range(columns):
        part = slice(c * LEV, (c + 1) * LEV)
        count = counts_ref[:, c : c + 1]
        inner = (down == across) & (down + 1 < count)
        face = jnp.sum(jnp.where(inner, level_face_ref[c : c + 1, :], 0.0), axis=1, keepdims=True)
        face_ref[part, :] = jnp.broadcast_to(face, (LEV, R))
        live_ref[part, :] = jnp.where(level < count, 1.0, 0.0)
    later()
    diff_ref[...] = diffuse_rows(modes_ref[...], face_ref)


def first_kernel(plan, *allrefs):
    chem_in, chem, sems = allrefs[:4], allrefs[-5:-1], allrefs[-1]
    diff_ref, emis_ref, live_ref, *refs, field_ref = allrefs[4:-5]
    ready = fetch(chem_in, chem, sems)
    if plan:
        chip_ref, mine_ref, theirs_ref, tend_ref, rate_ref, top_ref, coef_ref = refs
        rows = chip_ref.shape[0]
        place = lax.axis_index("col")
        chip, side = place // 2, place % 2
        for j, pair in enumerate(plan):
            for ref, mask in (
                (mine_ref, jnp.where(side == 0, pair[0], pair[1])),
                (theirs_ref, jnp.where(side == 0, pair[1], pair[0])),
            ):
                spot = pl.multiple_of((chip ^ mask) * rows, rows)
                coef_ref[pl.ds(spot, rows), :] = ref[j * rows : (j + 1) * rows, :]
        coef_ref[pl.ds(pl.multiple_of(chip * rows, rows), rows), :] = chip_ref[...]
    else:
        coef_ref, tend_ref, rate_ref, top_ref = refs
    react(
        diff_ref[...], half_start(tend_ref.shape[1], False), coef_ref, emis_ref, live_ref,
        ready, *chem, field_ref, tend_ref, rate_ref, top_ref,
    )


def second_kernel(
    pair_in_ref, stoich_in_ref, speed_in_ref, loss_in_ref,
    diff_ref, emis_ref, live_ref, coef_ref,
    tend_ref, rate_ref, top_ref,
    field_ref, *chem_sems,
):
    *chem, sems = chem_sems
    ready = fetch((pair_in_ref, stoich_in_ref, speed_in_ref, loss_in_ref), chem, sems)
    react(
        diff_ref[...], half_start(tend_ref.shape[1], True), coef_ref, emis_ref, live_ref,
        ready, *chem, field_ref, tend_ref, rate_ref, top_ref,
    )


STEP = TIME_STEP * math.sqrt(R)


def ready_kernel(
    diff_ref, pull_ref, solve_ref, base_ref, diff_high_ref, diff_low_ref, high_ref, low_ref
):
    diffused = diff_ref[...]
    base_ref[...] = diffused + STEP * pull_ref[...]
    diff_high_ref[...], diff_low_ref[...] = split(diffused)
    high_ref[...], low_ref[...] = split(solve_ref[...])


def advance(base_ref, diff_high_ref, diff_low_ref, high_ref, low_ref, rate):
    transfer = mm3(split(rate), (high_ref[...], low_ref[...]), TN)
    moved = mm3((diff_high_ref[...], diff_low_ref[...]), split(transfer))
    return base_ref[...] - STEP * moved


def middle_kernel(
    total_rows,
    pair_in_ref, stoich_in_ref, speed_in_ref, loss_in_ref,
    base_ref, diff_high_ref, diff_low_ref, high_ref, low_ref,
    sum_ref, coef_ref, face_ref, emis_ref, live_ref,
    diff_ref, tend_ref, rate_ref, top_ref, coef_out_ref,
    field_ref, *chem_sems,
):
    *chem, sems = chem_sems
    ready = fetch((pair_in_ref, stoich_in_ref, speed_in_ref, loss_in_ref), chem, sems)
    raw = sum_ref[...]
    coef_out_ref[...] = (
        coef_ref[...].astype(F32) + RATE_STEP * (raw * (math.sqrt(R) / total_rows))
    ).astype(BF16)
    modes = advance(
        base_ref, diff_high_ref, diff_low_ref, high_ref, low_ref, raw * (1.0 / total_rows)
    )
    diffused = diffuse_rows(modes, face_ref)
    diff_ref[...] = diffused
    react(
        diffused, half_start(tend_ref.shape[1], False), coef_out_ref, emis_ref, live_ref,
        ready, *chem, field_ref, tend_ref, rate_ref, top_ref,
    )


def last_kernel(
    total_rows,
    base_ref, diff_high_ref, diff_low_ref, high_ref, low_ref,
    sum_ref, coef_ref,
    modes_ref, coef_out_ref,
):
    mine = coef_out_ref.shape[0]
    own = pl.ds(pl.multiple_of(lax.axis_index("col") * mine, mine), mine)
    coef_out_ref[...] = (
        coef_ref[own, :].astype(F32)
        + RATE_STEP * (sum_ref[own, :] * (math.sqrt(R) / total_rows))
    ).astype(BF16)
    modes_ref[...] = advance(
        base_ref, diff_high_ref, diff_low_ref, high_ref, low_ref,
        sum_ref[...] * (1.0 / total_rows),
    )


def identity():
    return (
        lax.broadcasted_iota(jnp.int32, (R, R), 0) == lax.broadcasted_iota(jnp.int32, (R, R), 1)
    ).astype(F32)


def widen(room):
    spread = room * (2.0 - room)
    return 2.0 * spread / (1.0 + spread), 2.0 / (1.0 + spread)


def refine(eye, high_ref, low_ref, inv_ref, room):
    room, factor = widen(room)
    inv = inv_ref[...]
    halves = split(inv)
    rest = eye - mm3((high_ref[...], low_ref[...]), halves)
    inv_ref[...] = factor * (inv + mm3(halves, split(rest)))
    return room


def inverse_start(ridge, steps, coef_ref, high_ref, low_ref, inv_ref, room_ref):
    coef = coef_ref[...]
    eye = identity()
    gram = mm(coef, coef, TN) + ridge * eye
    top = jnp.max(jnp.sum(jnp.abs(gram), axis=0, keepdims=True))
    high_ref[...], low_ref[...] = split(gram)
    scale = 2.0 / (top + ridge)
    room, factor = widen(ridge * scale)
    inv_ref[...] = (factor * scale) * (2.0 * eye - scale * gram)
    room = lax.fori_loop(
        0, steps, lambda i, room: refine(eye, high_ref, low_ref, inv_ref, room), room
    )
    room_ref[...] = jnp.full(room_ref.shape, room, F32)


def inverse_end(
    room_in_ref, high_ref, low_ref, inv_in_ref, coef_ref, give_ref, keep_ref,
    solve_ref, pull_ref, inv_ref,
):
    eye = identity()
    inv_ref[...] = inv_in_ref[...]
    lax.while_loop(
        lambda room: room < 1.0 - 1e-5,
        lambda room: refine(eye, high_ref, low_ref, inv_ref, room),
        jnp.max(room_in_ref[...]),
    )
    coef = coef_ref[...]
    high, low = split(inv_ref[...])
    solve = mm(coef, high) + mm(coef, low)
    solve_ref[...] = solve
    half = give_ref.shape[1]
    parts = []
    for ref, keep in ((give_ref, False), (keep_ref, True)):
        start = pl.multiple_of(half_start(half, keep), half)
        high, low = split(solve_ref[pl.ds(start, half), :])
        parts.append(mm(ref[...], high) + mm(ref[...], low))
    pull_ref[...] = parts[0] + parts[1]


VMEM_LIMIT = 48 * 1024 * 1024


def call(kernel, n_hbm, outs, scratch, *args):
    args = [
        pltpu.with_memory_space_constraint(arg, pltpu.HBM) if i < n_hbm else arg
        for i, arg in enumerate(args)
    ]
    return pl.pallas_call(
        kernel,
        in_specs=[
            pl.BlockSpec(memory_space=pltpu.HBM if i < n_hbm else pltpu.VMEM)
            for i in range(len(args))
        ],
        out_specs=[pl.BlockSpec(memory_space=pltpu.VMEM)] * len(outs),
        out_shape=[jax.ShapeDtypeStruct(shape, dtype) for shape, dtype in outs],
        scratch_shapes=scratch,
        compiler_params=pltpu.CompilerParams(vmem_limit_bytes=VMEM_LIMIT),
    )(*args)


def tied(value, first):
    return lax.optimization_barrier((first, value))[1]


def swap(value, n, masks):
    return lax.ppermute(value, "col", [(i, i ^ masks[i % 2]) for i in range(n) if masks[i % 2]])


EXTRA = 8
LIFT = 15.0


def encode(part, power):
    scaled = (part * jnp.exp2(LIFT - power)).astype(jnp.float16)
    powers = jnp.broadcast_to(power, (EXTRA, R)).astype(jnp.float16)
    return lax.optimization_barrier(jnp.concatenate([scaled, powers], 0))


def decode(message):
    rows = message.shape[0] - EXTRA
    power = message[rows : rows + 1].astype(F32)
    return message[:rows].astype(F32) * jnp.exp2(power - LIFT), power


def sum_over(give, top, keep_half, n, work, prepare):
    got = swap(jnp.concatenate([give, top], 0), n, (1, 1))
    keep, keep_top, state = keep_half()
    got, keep = lax.optimization_barrier((got, keep))
    half = give.shape[0]
    side = lax.axis_index("col") & 1
    part = keep + got[:half]
    power = jnp.maximum(keep_top[:1], got[half : half + 1]) + 1.0
    work = list(work)
    mask = 2
    while mask < n:
        masks = [mask, mask * 2, mask * 3] if mask * 2 < n else [mask]
        message = encode(part, power)
        others = [swap(message, n, (m, m)) for m in masks]
        mask *= 4 if len(masks) == 3 else 2
        while work:
            state = work.pop(0)(state, message)
            others, state = lax.optimization_barrier((others, state))
            if mask < n:
                break
        part, power = decode(message)
        for other in others:
            more, high = decode(other)
            part = part + more
            power = jnp.maximum(power, high)
        power = power + float(len(masks))
    other = swap(part, n, (1, 1))
    state = prepare(state, part)
    other, state = lax.optimization_barrier((other, state))
    total = jnp.where(
        side == 0, jnp.concatenate([part, other], 0), jnp.concatenate([other, part], 0)
    )
    return total, state


def on_device(
    mode_rows,
    coeffs,
    diffusivity,
    counts,
    emis_idx,
    emis_table,
    reactants,
    stoich,
    rate_consts,
    loss_rates,
):
    n = lax.axis_size("col")
    rows = mode_rows.shape[0]
    total_rows = rows * n
    mine = coeffs.shape[0]
    members = mine * n
    columns = counts.shape[0]
    ridge = RIDGE_SHARE * members
    half = members // 2
    block = math.gcd(half, 256)
    rows_f32 = ((rows, R), F32)
    rows_bf = ((rows, R), BF16)
    tend_out = ((rows, half), BF16)
    half_out = ((half, R), F32)
    rate_out = ((members, R), F32)
    top_out = ((EXTRA, R), F32)
    coef_out = ((members, R), BF16)
    tables = (reactants.T, stoich.T, rate_consts.reshape(1, NREAC), loss_rates.reshape(1, S))
    react_tmp = [
        pltpu.VMEM((rows, block), F32),
        *(pltpu.SMEM(value.shape, value.dtype) for value in tables),
        pltpu.SemaphoreType.DMA((len(tables),)),
    ]
    square = ((R, R), F32)
    square_bf = ((R, R), BF16)

    def stage(modes):
        by_level = ((columns * LEV, R), F32)
        index = emis_idx.reshape(1, members)
        *chem, diff, emis, face, live = call(
            functools.partial(stage_kernel, columns), 8,
            [(value.shape, value.dtype) for value in tables]
            + [rows_f32, ((S, members), F32), by_level, by_level],
            [
                pltpu.SMEM((S, NEMIS), F32),
                pltpu.VMEM(diffusivity.shape, F32),
                pltpu.VMEM((1, members), jnp.int32),
                pltpu.VMEM((rows, R), F32),
                pltpu.SemaphoreType.DMA((8,)),
            ],
            *tables, emis_table.T, diffusivity, index, modes, counts.reshape(1, columns),
        )
        return chem, diff, emis, face, live

    if n == 16:
        plan = ((1, 1), (2, 3), (4, 6), (5, 7))
        other = swap(coeffs, n, (1, 1))
        side = lax.axis_index("col") & 1
        chip = jnp.where(
            side == 0, jnp.concatenate([coeffs, other], 0), jnp.concatenate([other, coeffs], 0)
        )
        fetched = [swap(chip, n, (2 * a, 2 * b)) for a, b in plan]
        chem, diff, emis, face, live = stage(tied(mode_rows, chip))
        fetched, diff = lax.optimization_barrier((fetched, diff))
        mine_rows = jnp.concatenate(fetched, 0)
        theirs = swap(mine_rows, n, (1, 1))
        gathered = (chip, mine_rows, theirs)
        tend, rate, top, coef = call(
            functools.partial(first_kernel, plan), 0,
            [tend_out, half_out, top_out, coef_out], react_tmp,
            *chem, diff, emis, live, *gathered,
        )
    else:
        coef = lax.all_to_all(jnp.tile(coeffs, (n, 1)), "col", 0, 0, tiled=True)
        chem, diff, emis, face, live = stage(mode_rows)
        tend, rate, top = call(
            functools.partial(first_kernel, ()), 0,
            [tend_out, half_out, top_out], react_tmp,
            *chem, diff, emis, live, coef,
        )

    def summed(rate, top, coef, tend, diff):
        def keep_half():
            tend_keep, keep, keep_top = call(
                second_kernel, 0, [tend_out, half_out, top_out], react_tmp,
                *chem, tied(diff, rate), emis, live, coef,
            )
            return keep, keep_top, tend_keep

        def start(tend_keep, ready):
            return tend_keep, call(
                functools.partial(inverse_start, ridge, 4), 0,
                [square_bf, square_bf, square, top_out], [], tied(coef, ready),
            )

        def end(state, ready):
            tend_keep, (high, low, inv, gap) = tied(state, ready)
            return call(
                inverse_end, 0, [rate_out, rows_f32], [pltpu.VMEM((R, R), F32)],
                gap, high, low, inv, coef, tend, tend_keep,
            )

        def prepare(state, ready):
            solved, pull = tied(state, ready)
            return call(
                ready_kernel, 0,
                [rows_f32, rows_bf, rows_bf, ((members, R), BF16), ((members, R), BF16)], [],
                diff, pull, solved,
            )

        return sum_over(rate, top, keep_half, n, (start, end), prepare)

    for _ in range(NSUB - 1):
        total, prepared = summed(rate, top, coef, tend, diff)
        diff, tend, rate, top, coef = call(
            functools.partial(middle_kernel, total_rows), 0,
            [rows_f32, tend_out, half_out, top_out, coef_out], react_tmp,
            *chem, *prepared, total, coef, face, emis, live,
        )
    total, prepared = summed(rate, top, coef, tend, diff)
    return tuple(
        call(
            functools.partial(last_kernel, total_rows), 0,
            [rows_f32, ((mine, R), BF16)], [],
            *prepared, total, coef,
        )
    )


def solution(mesh):
    placed = (
        P(("grp", "col"), None),
        P(("grp", "col"), None),
        P(("grp", "col"), None),
        P(("grp", "col")),
        P("grp"),
        P(),
        P(),
        P(),
        P(),
        P(),
    )
    return jax.shard_map(
        on_device,
        mesh=mesh,
        in_specs=placed,
        out_specs=(P(("grp", "col"), None), P(("grp", "col"), None)),
        check_vma=False,
    )
```
